768 devices in a mesh: rows: 192 (over x, z_hi, y, core), cols: 4 (over z_lo).
Axes of the slice: x: 4, y: 8, z: 12 (z_hi: 3, z_lo: 4; z = z_hi * 4 + z_lo), core: 2. Of those that a mesh axis runs over, the one named last changes fastest.
Arguments:
- frames: bfloat16 [2, 64, 3072, 512], P(None, None, 'rows', 'cols'), may hold values from -6 to 6
- hidden_state: bfloat16 [64, 3072, 512], P(None, 'rows', 'cols'), may hold values from -1 to 1
- cell_state: float32 [64, 3072, 512], P(None, 'rows', 'cols'), may hold values from -6 to 6
- depth_kernel: float32 [128, 3, 3], replicated, may hold values from -3 to 3
- point_weight: bfloat16 [256, 128], replicated, may hold values from -0.5 to 0.5
- gate_bias: float32 [256], replicated, may hold values from -3 to 3
- mixing_weight: bfloat16 [192, 64], replicated, may hold values from -0.75 to 0.75
- query_gain: float32 [64], replicated, may hold values from 0.2 to 40
- output_weight: bfloat16 [64, 64], replicated, may hold values from -0.75 to 0.75
Outputs:
- hidden_final: bfloat16 [64, 3072, 512], P(None, 'rows', 'cols')
- cell_final: float32 [64, 3072, 512], P(None, 'rows', 'cols')
- attended: float32 [2, 64, 384, 64], P(None, None, 'rows', 'cols')
The draws below stay inside these ranges and needn't reach their ends.
All inputs are finite; a program needn't handle non-finite values.
Results may differ from the reference program's by a relative error of at most 0.0065.
Values may be sent and summed in bfloat16 or wider, within the bound.
A program may use at most 128 MiB of HBM per device.

```python
import math
import jax
import jax.numpy as jnp
from jax import lax

CIN = 64
CH = 64
HEAD_DIM = 64
LEADS = 2
R_DEV = 16
NR = 3072
NC = 512
N_ROWS = 192


def draw_query_gain(key, part):
    return jnp.exp(jax.random.uniform(key, (HEAD_DIM,), jnp.float32, math.log(2.0), math.log(20.0)))


def levels(own_key, extent, cuts, least, high):
    gain, own = 1.0, jax.random.fold_in(own_key, 6)
    for position, shards_of in cuts:
        steps = jnp.exp(jax.random.uniform(jax.random.fold_in(own, position), (shards_of,), jnp.float32, least / len(cuts), high / len(cuts)))
        gain = gain * jnp.repeat(steps, extent[position] // shards_of).reshape([-1 if axis == position else 1 for axis in range(len(extent))])
    return gain


def gaussian(rng, extent, spread, limit, pieces=(), held_as=jnp.bfloat16):
    loudness = levels(rng, extent, pieces, -0.22, 0.18) if pieces else 1.0
    drawn = jax.random.normal(rng, extent, jnp.float32) * spread * loudness
    return jnp.minimum(jnp.maximum(drawn, -limit), limit).astype(held_as)


def setup_inputs(seed: int = 0) -> dict:
    streams_of = jax.random.split(jax.random.key(seed), 10)
    frames = gaussian(streams_of[0], (LEADS, CIN, NR, NC), 1.0, 6.0, ((2, 192), (3, 4)))
    hidden_state = jnp.clip(jax.random.uniform(streams_of[1], (CH, NR, NC), jnp.float32, -1.0, 1.0) * levels(streams_of[1], (CH, NR, NC), ((1, 192), (2, 4)), -0.4, 0.0), -1.0, 1.0).astype(jnp.bfloat16)
    cell_state = gaussian(streams_of[2], (CH, NR, NC), 1.0, 6.0, ((1, 192), (2, 4)), jnp.float32)
    depth_kernel = gaussian(streams_of[3], (CIN + CH, 3, 3), 0.33, 3.0, (), jnp.float32)
    point_weight = gaussian(streams_of[4], (4 * CH, CIN + CH), (CIN + CH) ** -0.5, 0.5)
    gate_bias = gaussian(streams_of[5], (4 * CH,), 0.5, 3.0, (), jnp.float32)
    mixing_weight = gaussian(streams_of[6], (3 * HEAD_DIM, CH), CH ** -0.5, 0.75)
    query_gain = draw_query_gain(jax.random.fold_in(streams_of[9], 71), 0)
    output_weight = gaussian(streams_of[8], (CH, HEAD_DIM), HEAD_DIM ** -0.5, 0.75)
    return dict(frames=frames, hidden_state=hidden_state, cell_state=cell_state, depth_kernel=depth_kernel, point_weight=point_weight, gate_bias=gate_bias, mixing_weight=mixing_weight, query_gain=query_gain, output_weight=output_weight)


def depthwise(portion, depth_kernel, row_count, col_count):
    summed = None
    for a in range(3):
        for b in range(3):
            addend = depth_kernel[:, a, b][:, None, None] * portion[:, a:a + row_count, b:b + col_count]
            summed = addend if summed is None else summed + addend
    return summed

def recurrence(gates, previous):
    channels = previous.shape[0]
    in_gate = gates[:channels]
    forget = gates[channels:2 * channels]
    out_gate = gates[2 * channels:3 * channels]
    candidate = gates[3 * channels:]
    memory = jax.nn.sigmoid(forget) * previous + jax.nn.sigmoid(in_gate) * jnp.tanh(candidate)
    hidden = (jax.nn.sigmoid(out_gate) * jnp.tanh(memory)).astype(jnp.bfloat16)
    return (hidden, memory)

def normalize(vectors, axis):
    return vectors * lax.rsqrt(lax.optimization_barrier(jnp.mean(vectors * vectors, axis=axis, keepdims=True)) + 1e-06)

def lead_step(frame, hidden, memory, depth_kernel, point_weight, gate_bias):
    stacked = jnp.concatenate([frame, hidden], axis=0)
    padded = jnp.pad(stacked, ((0, 0), (1, 1), (1, 1)))
    col_count = stacked.shape[2]
    channels = hidden.shape[0]

    def one_band(band_index):
        first_row = (band_index * R_DEV).astype(jnp.int32)
        portion = lax.dynamic_slice_in_dim(padded, first_row, R_DEV + 2, 1).astype(jnp.float32)
        spatial = depthwise(portion, depth_kernel, R_DEV, col_count).astype(jnp.bfloat16)
        gates = jnp.dot(point_weight, spatial.reshape(spatial.shape[0], -1), preferred_element_type=jnp.float32)
        gates = gates.reshape(-1, R_DEV, col_count) + gate_bias[:, None, None]
        previous = lax.dynamic_slice_in_dim(memory, first_row, R_DEV, 1)
        return recurrence(gates, previous)
    hiddens, memories = lax.map(one_band, jnp.arange(N_ROWS, dtype=jnp.int32))
    hidden_new = jnp.transpose(hiddens, (1, 0, 2, 3)).reshape(channels, -1, col_count)
    memory_new = jnp.transpose(memories, (1, 0, 2, 3)).reshape(channels, -1, col_count)
    return (hidden_new, memory_new)

def attend(hidden, mixing_weight, query_gain, output_weight):
    channels, row_count, col_count = hidden.shape
    head_dim = query_gain.shape[0]
    pooled = hidden.astype(jnp.float32).reshape(channels, row_count // 8, 8, col_count // 8, 8).mean(axis=(2, 4)).astype(jnp.bfloat16)
    pool_rows, pool_cols = (pooled.shape[1], pooled.shape[2])
    projected = jnp.dot(mixing_weight, pooled.reshape(channels, -1), preferred_element_type=jnp.float32)
    queries = (normalize(projected[:head_dim], 0) * query_gain[:, None]).astype(jnp.bfloat16)
    key_rows = normalize(projected[head_dim:2 * head_dim], 0).astype(jnp.bfloat16)
    value_rows = projected[2 * head_dim:].astype(jnp.bfloat16)
    queries = queries.reshape(head_dim, pool_rows, pool_cols).astype(jnp.float32)
    key_rows = key_rows.reshape(head_dim, pool_rows, pool_cols).astype(jnp.float32)
    value_rows = value_rows.reshape(head_dim, pool_rows, pool_cols).astype(jnp.float32)
    scores = jnp.einsum('dpc,dqc->cpq', queries, key_rows) / math.sqrt(head_dim)
    weights = jax.nn.softmax(scores, axis=-1)
    mixed = jnp.einsum('cpq,dqc->dpc', weights, value_rows).astype(jnp.bfloat16)
    update = jnp.dot(output_weight, mixed.reshape(head_dim, -1), preferred_element_type=jnp.float32)
    return pooled.astype(jnp.float32) + update.reshape(channels, pool_rows, pool_cols)

def reference(frames, hidden_state, cell_state, depth_kernel, point_weight, gate_bias, mixing_weight, query_gain, output_weight):
    hidden, memory = (hidden_state, cell_state)
    results = []
    for horizon in range(LEADS):
        hidden, memory = lead_step(frames[horizon], hidden, memory, depth_kernel, point_weight, gate_bias)
        results.append(attend(hidden, mixing_weight, query_gain, output_weight))
    return (hidden, memory, jnp.stack(results))
```

```python
import functools
import math

import jax
import jax.numpy as jnp
from jax import lax
from jax.experimental import pallas as pl
from jax.experimental.pallas import tpu as pltpu
from jax.sharding import PartitionSpec as P

LEADS = 2
MESH = pl.DeviceIdType.MESH


def with_halo(cells, sides, width):
    for axis, dim in sides:
        count = lax.axis_size(axis)
        ends = count - 1
        head = lax.slice_in_dim(cells, 0, width, axis=dim)
        tail = lax.slice_in_dim(cells, cells.shape[dim] - width, cells.shape[dim], axis=dim)
        cells = jnp.concatenate(
            [
                lax.ppermute(tail, axis, [(i, (i + 1) % count) for i in range(ends)]),
                cells,
                lax.ppermute(head, axis, [((i + 1) % count, i) for i in range(ends)]),
            ],
            axis=dim,
        )
    return cells


def depthwise(portion, depth_kernel, row_count, col_count):
    summed = None
    for a in range(3):
        for b in range(3):
            addend = (
                depth_kernel[:, a, b][:, None, None]
                * portion[:, a : a + row_count, b : b + col_count]
            )
            summed = addend if summed is None else summed + addend
    return summed


def recurrence(gates, previous):
    channels = previous.shape[0]
    in_gate = gates[:channels]
    forget = gates[channels : 2 * channels]
    out_gate = gates[2 * channels : 3 * channels]
    candidate = gates[3 * channels :]
    memory = jax.nn.sigmoid(forget) * previous + jax.nn.sigmoid(in_gate) * jnp.tanh(candidate)
    hidden = (jax.nn.sigmoid(out_gate) * jnp.tanh(memory)).astype(jnp.bfloat16)
    return (hidden, memory)


def gate_update(padded, memory, depth_kernel, point_weight, gate_bias):
    row_count, col_count = (memory.shape[1], memory.shape[2])
    spatial = depthwise(padded.astype(jnp.float32), depth_kernel, row_count, col_count).astype(
        jnp.bfloat16
    )
    gates = jnp.dot(
        point_weight, spatial.reshape(spatial.shape[0], -1), preferred_element_type=jnp.float32
    )
    gates = gates.reshape(-1, row_count, col_count) + gate_bias[:, None, None]
    return recurrence(gates, memory)


def lane_half(shape):
    return lax.broadcasted_iota(jnp.int32, shape, len(shape) - 1) < shape[-1] // 2


def half_norm(vectors, low):
    squares = vectors * vectors
    count = vectors.shape[-1] // 2
    first = jnp.sum(jnp.where(low, squares, 0.0), axis=-1, keepdims=True) / count
    second = jnp.sum(jnp.where(low, 0.0, squares), axis=-1, keepdims=True) / count
    return vectors * jnp.where(low, lax.rsqrt(first + 1e-06), lax.rsqrt(second + 1e-06))


def attend_column(own, every, qkv_weight, gain, out_weight):
    lanes = own.shape[-1]
    low = lane_half(own.shape)
    query = jnp.dot(own, qkv_weight[:, :lanes], preferred_element_type=jnp.float32)
    queries = half_norm(query, low) * gain
    turned = pltpu.roll(queries, lanes // 2, 1)
    stacked = jnp.concatenate(
        [
            jnp.where(low, queries, 0.0),
            jnp.where(low, turned, 0.0),
            jnp.where(low, 0.0, turned),
            jnp.where(low, 0.0, queries),
        ],
        axis=0,
    ).astype(jnp.bfloat16)
    key_value = jnp.dot(every, qkv_weight[:, lanes:], preferred_element_type=jnp.float32)
    keys = half_norm(key_value[:, :lanes], lane_half(every.shape)).astype(jnp.bfloat16)
    values = key_value[:, lanes:].astype(jnp.bfloat16)
    scores = lax.dot_general(
        stacked, keys, (((1,), (1,)), ((), ())), preferred_element_type=jnp.float32
    ) * (1.0 / math.sqrt(lanes // 2))
    count = own.shape[0]
    highest = jnp.max(scores, axis=1, keepdims=True)
    highest = jnp.maximum(highest[: 2 * count], highest[2 * count :])
    weights = jnp.exp(scores - jnp.concatenate([highest, highest], axis=0))
    mass = jnp.sum(weights, axis=1, keepdims=True)
    mass = mass[: 2 * count] + mass[2 * count :]
    weighted = jnp.dot(weights.astype(jnp.bfloat16), values, preferred_element_type=jnp.float32)
    swapped = pltpu.roll(weighted, lanes // 2, 1)
    mixed = jnp.where(
        low,
        (weighted[:count] + swapped[2 * count : 3 * count]) / mass[:count],
        (swapped[count : 2 * count] + weighted[3 * count :]) / mass[count:],
    )
    update = jnp.dot(mixed.astype(jnp.bfloat16), out_weight, preferred_element_type=jnp.float32)
    return own.astype(jnp.float32) + update


def attention_kernel(
    groups,
    members,
    pooled_ref,
    qkv_ref,
    gain_ref,
    out_weight_ref,
    out_ref,
    column,
    gathered,
    result,
    send_a,
    recv_a,
    send_b,
    recv_b,
    send_c,
    recv_c,
):
    me = lax.axis_index("rows")
    group, member = me // members, me % members

    def mate(step):
        return group * members + (member + step) % members

    def twin(step):
        return ((group + step) % groups) * members + member

    barrier = pltpu.get_barrier_semaphore()
    for step in range(1, members):
        pl.semaphore_signal(barrier, inc=1, device_id={"rows": mate(step)}, device_id_type=MESH)
    for step in range(1, groups):
        pl.semaphore_signal(barrier, inc=1, device_id={"rows": twin(step)}, device_id_type=MESH)
    pl.semaphore_wait(barrier, members + groups - 2)

    copies = []
    for step in range(1, members):
        target = (member + step) % members
        copies.append(
            pltpu.make_async_remote_copy(
                src_ref=pooled_ref.at[target],
                dst_ref=column.at[member],
                send_sem=send_a.at[step],
                recv_sem=recv_a.at[step],
                device_id={"rows": mate(step)},
                device_id_type=MESH,
            )
        )
        copies[-1].start()
    column[member] = pooled_ref[member]
    for copy in copies:
        copy.wait()
    for lead in range(LEADS):
        gathered[lead, group] = column[:, lead, :].astype(jnp.bfloat16)
    copies = []
    for step in range(1, groups):
        copies.append(
            pltpu.make_async_remote_copy(
                src_ref=gathered.at[:, group],
                dst_ref=gathered.at[:, group],
                send_sem=send_b.at[step],
                recv_sem=recv_b.at[step],
                device_id={"rows": twin(step)},
                device_id_type=MESH,
            )
        )
        copies[-1].start()
    for copy in copies:
        copy.wait()
    for lead in range(LEADS):
        result[:, lead, :] = attend_column(
            gathered[lead, group],
            gathered[lead].reshape(groups * members, -1),
            qkv_ref[...],
            gain_ref[...],
            out_weight_ref[...],
        )
    copies = []
    for step in range(1, members):
        target = (member + step) % members
        copies.append(
            pltpu.make_async_remote_copy(
                src_ref=result.at[target],
                dst_ref=out_ref.at[member],
                send_sem=send_c.at[step],
                recv_sem=recv_c.at[step],
                device_id={"rows": mate(step)},
                device_id_type=MESH,
            )
        )
        copies[-1].start()
    out_ref[member] = result[member]
    for copy in copies:
        copy.wait()


def twice(weight):
    zeros = jnp.zeros_like(weight)
    return jnp.concatenate(
        [jnp.concatenate([weight, zeros], axis=1), jnp.concatenate([zeros, weight], axis=1)], axis=0
    )


def pool(hidden):
    channels, row_count, col_count = hidden.shape
    return (
        hidden.astype(jnp.float32)
        .reshape(channels, row_count // 8, 8, col_count // 8, 8)
        .mean(axis=(2, 4))
        .astype(jnp.bfloat16)
    )


def attend(pooled, mixing_weight, query_gain, output_weight):
    leads, channels, pool_rows, members = pooled.shape
    groups = lax.axis_size("rows") // members
    head_dim = query_gain.shape[0]
    lanes = pool_rows * channels
    given = jnp.transpose(pooled, (3, 0, 2, 1)).reshape(members, leads, lanes).astype(jnp.float32)
    turned = mixing_weight.T
    qkv = jnp.concatenate(
        [twice(turned[:, k * head_dim : (k + 1) * head_dim]) for k in range(3)], axis=1
    )
    gain = jnp.concatenate([query_gain, query_gain])[None]
    dma = pltpu.SemaphoreType.DMA
    result = pl.pallas_call(
        functools.partial(attention_kernel, groups, members),
        out_shape=jax.ShapeDtypeStruct((members, leads, lanes), jnp.float32),
        in_specs=[pl.BlockSpec(memory_space=pltpu.VMEM)] * 4,
        out_specs=pl.BlockSpec(memory_space=pltpu.VMEM),
        scratch_shapes=[
            pltpu.VMEM((members, leads, lanes), jnp.float32),
            pltpu.VMEM((leads, groups, members, lanes), jnp.bfloat16),
            pltpu.VMEM((members, leads, lanes), jnp.float32),
            dma((members,)),
            dma((members,)),
            dma((groups,)),
            dma((groups,)),
            dma((members,)),
            dma((members,)),
        ],
        compiler_params=pltpu.CompilerParams(collective_id=0, has_side_effects=True),
    )(given, qkv, gain, twice(output_weight.T))
    return jnp.transpose(result.reshape(members, leads, pool_rows, channels), (1, 3, 2, 0))


def body(
    frames,
    hidden_state,
    cell_state,
    depth_kernel,
    point_weight,
    gate_bias,
    mixing_weight,
    query_gain,
    output_weight,
):
    hidden, memory = (hidden_state, cell_state)
    results = []
    for horizon in range(LEADS):
        stacked = jnp.concatenate([frames[horizon], hidden], axis=0)
        padded = with_halo(stacked, (("rows", 1), ("cols", 2)), 1)
        hidden, memory = gate_update(padded, memory, depth_kernel, point_weight, gate_bias)
        results.append(pool(hidden))
    attended = attend(jnp.stack(results), mixing_weight, query_gain, output_weight)
    return (hidden, memory, attended)


def solution(mesh):
    in_specs = (
        P(None, None, "rows", "cols"),
        P(None, "rows", "cols"),
        P(None, "rows", "cols"),
        P(),
        P(),
        P(),
        P(),
        P(),
        P(),
    )
    out_specs = (P(None, "rows", "cols"), P(None, "rows", "cols"), P(None, None, "rows", "cols"))
    return jax.shard_map(body, mesh=mesh, in_specs=in_specs, out_specs=out_specs, check_vma=False)
```

```python
import functools
import math

import jax
import jax.numpy as jnp
import numpy as np
from jax import lax
from jax.experimental import pallas as pl
from jax.experimental.pallas import tpu as pltpu
from jax.sharding import PartitionSpec as P

LEADS = 2
POOL = 8
MESH = pl.DeviceIdType.MESH
F32 = jnp.float32
BF16 = jnp.bfloat16
ROW_WAYS = (-1, 1)
EDGE_WAYS = tuple((dr, dc) for dr in (-1, 0, 1) for dc in (-1, 1))


def dot(left, right):
    return jnp.dot(left, right, preferred_element_type=F32)


def dot_t(left, right):
    return lax.dot_general(left, right, (((1,), (1,)), ((), ())), preferred_element_type=F32)


def lane_half(shape):
    return lax.broadcasted_iota(jnp.int32, shape, len(shape) - 1) < shape[-1] // 2


def half_norm(vectors, low):
    squares = vectors * vectors
    count = vectors.shape[-1] // 2
    first = jnp.sum(jnp.where(low, squares, 0.0), axis=-1, keepdims=True) / count
    second = jnp.sum(jnp.where(low, 0.0, squares), axis=-1, keepdims=True) / count
    return vectors * jnp.where(low, lax.rsqrt(first + 1e-06), lax.rsqrt(second + 1e-06))


def twice(weight):
    wide = jnp.concatenate([weight, weight], axis=1)
    low = lane_half(wide.shape)
    return jnp.concatenate([jnp.where(low, wide, 0.0), jnp.where(low, 0.0, wide)], axis=0)


def attend_column(own, every, mix_ref, gain, out_weight):
    lanes = own.shape[-1]
    low = lane_half(own.shape)
    queries = half_norm(dot_t(own, mix_ref[0]), low) * gain
    turned = pltpu.roll(queries, lanes // 2, 1)
    stacked = jnp.concatenate(
        [
            jnp.where(low, queries, 0.0),
            jnp.where(low, turned, 0.0),
            jnp.where(low, 0.0, turned),
            jnp.where(low, 0.0, queries),
        ],
        axis=0,
    ).astype(BF16)
    keys = half_norm(dot_t(every, mix_ref[1]), lane_half(every.shape)).astype(BF16)
    values = dot_t(every, mix_ref[2]).astype(BF16)
    scores = dot_t(stacked, keys) * (1.0 / math.sqrt(lanes // 2))
    count = own.shape[0]
    highest = jnp.max(scores, axis=1, keepdims=True)
    highest = jnp.maximum(highest[: 2 * count], highest[2 * count :])
    weights = jnp.exp(scores - jnp.concatenate([highest, highest], axis=0))
    mass = jnp.sum(weights, axis=1, keepdims=True)
    mass = mass[: 2 * count] + mass[2 * count :]
    weighted = dot(weights.astype(BF16), values)
    swapped = pltpu.roll(weighted, lanes // 2, 1)
    mixed = jnp.where(
        low,
        (weighted[:count] + swapped[2 * count : 3 * count]) / mass[:count],
        (swapped[count : 2 * count] + weighted[3 * count :]) / mass[count:],
    )
    return own.astype(F32) + dot_t(mixed.astype(BF16), out_weight)


def depthwise(x_ref, taps_ref, spatial_ref, blocks, bands):
    cols = x_ref.shape[2]

    def block(index, carry):
        lo = pl.multiple_of(index * 16, 16)
        taps = [taps_ref[k, pl.ds(lo, 16), :][None] for k in range(9)]
        for start, count in bands:
            rows = x_ref[start : start + count + 2, pl.ds(lo, 16), :]
            left, middle, right = (
                taps[b] * rows[:count]
                + taps[3 + b] * rows[1 : count + 1]
                + taps[6 + b] * rows[2 : count + 2]
                for b in range(3)
            )
            lane = lax.broadcasted_iota(jnp.int32, (count * 16, cols), 1)
            left = pltpu.roll(left.reshape(count * 16, cols), 1, 1)
            right = pltpu.roll(right.reshape(count * 16, cols), cols - 1, 1)
            total = (
                jnp.where(lane == 0, 0.0, left)
                + middle.reshape(count * 16, cols)
                + jnp.where(lane == cols - 1, 0.0, right)
            ).astype(BF16)
            for j in range(count):
                row = start + j
                spatial_ref[row // 2, pl.ds(lo, 16), (row % 2) * cols : (row % 2 + 1) * cols] = (
                    total[j * 16 : (j + 1) * 16]
                )
        return carry

    lax.fori_loop(blocks[0], blocks[1], block, None)


def halo_column(frame_tiles, hidden_tiles, way, masks, taps_t, pad_ref):
    seen, above, below = masks
    first = 8 if way == 1 else 0
    slot = {dr: EDGE_WAYS.index((dr, way)) for dr in (-1, 0, 1)}

    def part(dr):
        frame = frame_tiles(slot[dr]).astype(F32)[first : first + 8]
        hidden = hidden_tiles(slot[dr]).astype(F32)[first : first + 8]
        low = lane_half(frame.shape)
        half = frame.shape[1] // 2
        upper = jnp.where(low, frame, pltpu.roll(hidden, half, 1))
        lower = jnp.where(low, pltpu.roll(frame, half, 1), hidden)
        return jnp.where(seen, upper, 0.0), jnp.where(seen, lower, 0.0)

    upper, lower = part(0)
    pad_ref[0:8] = jnp.where(above, part(1)[1], 0.0)
    pad_ref[8:16] = upper
    pad_ref[16:24] = lower
    pad_ref[24:32] = jnp.where(below, part(-1)[0], 0.0)
    b = 0 if way == 1 else 2
    return sum(taps_t[3 * a + b] * pad_ref[7 + a : 23 + a] for a in range(3))


def kernel(
    n_rows,
    n_cols,
    groups,
    members,
    frames_ref,
    hidden_ref,
    cell_ref,
    spread_ref,
    pick_ref,
    depth_ref,
    point_ref,
    bias_ref,
    mixing_ref,
    gain_ref,
    output_ref,
    hidden_out,
    cell_out,
    attended_out,
    frames_in,
    hidden_in,
    cell_now,
    plain,
    x0,
    x1,
    taps,
    spatial0,
    spatial1,
    weight,
    stacked,
    row_out0,
    row_in0,
    edge_out0,
    edge_in0,
    row_out1,
    row_in1,
    edge_out1,
    edge_in1,
    pad,
    mix,
    out_mix,
    given,
    column,
    gathered,
    result,
    returned,
    local_sem,
    send_row,
    recv_row,
    send_edge,
    recv_edge,
    send_a,
    recv_a,
    send_b,
    recv_b,
    send_c,
    recv_c,
):
    row, col = lax.axis_index("rows"), lax.axis_index("cols")
    group, member = row // members, row % members
    channels = hidden_in.shape[0] // 16
    both = 2 * channels
    cols = hidden_in.shape[1]

    def near(dr, dc):
        return ((row + dr + n_rows) % n_rows, (col + dc + n_cols) % n_cols)

    def mate(step):
        return (group * members + (member + step) % members, col)

    def twin(step):
        return (((group + step) % groups) * members + member, col)

    loads = [
        pltpu.make_async_copy(frames_ref.at[0], frames_in.at[0], local_sem.at[0]),
        pltpu.make_async_copy(hidden_ref, hidden_in, local_sem.at[1]),
        pltpu.make_async_copy(frames_ref.at[1], frames_in.at[1], local_sem.at[2]),
        pltpu.make_async_copy(cell_ref, cell_now, local_sem.at[3]),
        pltpu.make_async_copy(spread_ref, spatial0.at[:, both:], local_sem.at[4]),
        pltpu.make_async_copy(spread_ref, spatial1.at[:, both:], local_sem.at[5]),
    ]
    for load in loads:
        load.start()

    barrier = pltpu.get_barrier_semaphore()
    peers = [near(dr, 0) for dr in ROW_WAYS] + [near(dr, dc) for dr, dc in EDGE_WAYS]
    peers += [twin(step) for step in range(1, groups)] + [mate(step) for step in range(1, members)]
    for peer in peers:
        pl.semaphore_signal(barrier, inc=1, device_id=peer, device_id_type=MESH)

    pick_edges = pick_ref[16:, :]
    for k, (source, load) in enumerate(
        ((frames_in.at[0], loads[0]), (hidden_in, loads[1]), (frames_in.at[1], loads[2]))
    ):
        load.wait()
        plain[...] = source[...].astype(F32)
        target, base = ((x0, 0), (x0, channels), (x1, 0))[k]
        for r in range(16):
            plane = plain[pl.ds(r, channels, stride=16), :]
            target[r + 1, base : base + channels, :] = plane
            low = plane.astype(BF16)
            stacked[
                (r // 8) * channels : (r // 8 + 1) * channels, (r % 8) * cols : (r % 8 + 1) * cols
            ] = low
            if r in (0, 15):
                row_out0[r // 15, k * channels : (k + 1) * channels, :] = low
        edge_out0[k] = dot_t(pick_edges, stacked[...]).astype(BF16)

    pl.semaphore_wait(barrier, len(peers))
    sends = []

    def send(source, target, send_sem, recv_sem, device):
        copy = pltpu.make_async_remote_copy(
            src_ref=source,
            dst_ref=target,
            send_sem=send_sem,
            recv_sem=recv_sem,
            device_id=device,
            device_id_type=MESH,
        )
        copy.start()
        sends.append(copy)
        return copy

    def send_halo(step, row_out, row_in, edge_out, edge_in):
        copies = []
        for k, dr in enumerate(ROW_WAYS):
            copies.append(
                send(
                    row_out.at[k],
                    row_in.at[k],
                    send_row.at[step, k],
                    recv_row.at[step, k],
                    near(dr, 0),
                )
            )
        for k, (dr, dc) in enumerate(EDGE_WAYS):
            copies.append(
                send(
                    edge_out,
                    edge_in.at[k],
                    send_edge.at[step, k],
                    recv_edge.at[step, k],
                    near(dr, dc),
                )
            )
        return copies

    halo0 = send_halo(0, row_out0, row_in0, edge_out0, edge_in0)

    depth = depth_ref[...]
    for k in range(9):
        taps[k] = jnp.broadcast_to(depth[:, k : k + 1], (both, cols))
    taps_t = {k: jnp.transpose(taps[k])[0:1] for k in range(9) if k % 3 != 1}
    lane = lax.broadcasted_iota(jnp.int32, (4 * channels, cols), 1)
    sublane = lax.broadcasted_iota(jnp.int32, (4 * channels, cols), 0)
    halve = jnp.where(sublane < 3 * channels, 0.5, 1.0)
    bias = jnp.transpose(jnp.broadcast_to(bias_ref[...], (cols, 4 * channels))) * halve
    weight[:, :both] = (point_ref[...].astype(F32) * halve).astype(BF16)
    for part in range(3):
        rounded = bias.astype(BF16).astype(F32)
        bias_lanes = rounded if part == 0 else jnp.where(lane == 64 + part, rounded, bias_lanes)
        bias = bias - rounded
    bias_lanes = jnp.where(lane < 67, bias_lanes, 0.0)
    for k in range(3):
        mix[k] = twice(mixing_ref[k * channels : (k + 1) * channels, :].astype(F32)).astype(BF16)
    out_mix[...] = twice(output_ref[...].astype(F32)).astype(BF16)
    gain = jnp.concatenate([gain_ref[...], gain_ref[...]], axis=1)

    above, below = row > 0, row < n_rows - 1
    interior, rim = ((1, 4), (5, 4), (9, 4), (13, 2)), ((0, 1), (15, 1))
    whole = channels // 16
    depthwise(x0, taps, spatial0, (0, 2 * whole), interior)
    depthwise(x1, taps, spatial1, (0, whole), interior)

    def fill_rows(x_ref, base, row_in, offset):
        x_ref[0, base : base + channels, :] = jnp.where(
            above, row_in[1, offset : offset + channels, :].astype(F32), 0.0
        )
        x_ref[17, base : base + channels, :] = jnp.where(
            below, row_in[0, offset : offset + channels, :].astype(F32), 0.0
        )

    def extend(frame_tiles, hidden_tiles):
        left = halo_column(frame_tiles, hidden_tiles, 1, (col > 0, above, below), taps_t, pad)
        right = halo_column(
            frame_tiles, hidden_tiles, -1, (col < n_cols - 1, above, below), taps_t, pad
        )
        rest = jnp.zeros((cols - 64, both), F32)
        added = jnp.concatenate([left, right, left, right, rest], axis=0).astype(BF16)
        lifted = dot_t(weight[:, :both], added)
        rounded = lifted.astype(BF16).astype(F32)
        weight[:, both:] = jnp.where(
            lane < 32, rounded, jnp.where(lane < 64, lifted - rounded, bias_lanes)
        ).astype(BF16)

    def update(step, spatial):
        for pair in range(8):
            gates = dot(weight[...], spatial[pair])
            for j in range(2):
                r = 2 * pair + j
                in_gate, forget, out_gate, candidate = (
                    jnp.tanh(gates[k * channels : (k + 1) * channels, j * cols : (j + 1) * cols])
                    for k in range(4)
                )
                place = pl.ds(r, channels, stride=16)
                memory = (0.5 * forget + 0.5) * cell_now[place, :] + (
                    0.5 * in_gate + 0.5
                ) * candidate
                cell_now[place, :] = memory
                hidden = (0.5 * out_gate + 0.5) * jnp.tanh(memory)
                low = hidden.astype(BF16)
                stacked[
                    (r // 8) * channels : (r // 8 + 1) * channels,
                    (r % 8) * cols : (r % 8 + 1) * cols,
                ] = low
                if step == 0:
                    x1[r + 1, channels:both, :] = low.astype(F32)
                    if r in (0, 15):
                        row_out1[r // 15] = low
                else:
                    plain[place, :] = hidden

    def share(lead, pooled):
        given[lead, :, 0, :] = pooled.astype(BF16).astype(F32)
        column[lead, member] = given[lead, member]
        copies = []
        for step in range(1, members):
            copies.append(
                send(
                    given.at[lead, (member + step) % members],
                    column.at[lead, member],
                    send_a.at[lead, step],
                    recv_a.at[lead, step],
                    mate(step),
                )
            )
        return copies

    def gather(lead, copies):
        for copy in copies:
            copy.wait_recv()
        gathered[lead, group] = column[lead, :, 0, :].astype(BF16)
        copies = []
        for step in range(1, groups):
            copies.append(
                send(
                    gathered.at[lead, group],
                    gathered.at[lead, group],
                    send_b.at[lead, step],
                    recv_b.at[lead, step],
                    twin(step),
                )
            )
        return copies

    def attend(lead, copies):
        for copy in copies:
            copy.wait_recv()
        result[lead, :, 0, :] = attend_column(
            gathered[lead, group],
            gathered[lead].reshape(groups * members, both),
            mix,
            gain,
            out_mix[...],
        )
        returned[lead, member] = result[lead, member]
        copies = []
        for step in range(1, members):
            copies.append(
                send(
                    result.at[lead, (member + step) % members],
                    returned.at[lead, member],
                    send_c.at[lead, step],
                    recv_c.at[lead, step],
                    mate(step),
                )
            )
        return copies

    for copy in halo0:
        copy.wait_recv()
    fill_rows(x0, 0, row_in0, 0)
    fill_rows(x0, channels, row_in0, channels)
    depthwise(x0, taps, spatial0, (0, 2 * whole), rim)
    extend(lambda k: edge_in0[k, 0], lambda k: edge_in0[k, 1])
    for load in loads[3:]:
        load.wait()
    update(0, spatial0)
    picked = dot_t(pick_ref[...], stacked[...])
    edge_out1[...] = picked[16:].astype(BF16)
    halo1 = send_halo(1, row_out1, row_in1, edge_out1, edge_in1)
    shared0 = share(0, picked[:16])
    fill_rows(x1, 0, row_in0, both)
    depthwise(x1, taps, spatial1, (0, whole), rim)
    depthwise(x1, taps, spatial1, (whole, 2 * whole), interior)
    for copy in halo1:
        copy.wait_recv()
    fill_rows(x1, channels, row_in1, 0)
    depthwise(x1, taps, spatial1, (whole, 2 * whole), rim)
    extend(lambda k: edge_in0[k, 2], lambda k: edge_in1[k])
    gathered0 = gather(0, shared0)
    update(1, spatial1)
    picked = dot_t(pick_ref[:16, :], stacked[...])
    shared1 = share(1, picked)
    store_cell = pltpu.make_async_copy(cell_now, cell_out, local_sem.at[6])
    store_cell.start()
    hidden_in[...] = plain[...].astype(BF16)
    store_hidden = pltpu.make_async_copy(hidden_in, hidden_out, local_sem.at[7])
    store_hidden.start()
    returned0 = attend(0, gathered0)
    gathered1 = gather(1, shared1)
    returned1 = attend(1, gathered1)
    for lead, copies in enumerate((returned0, returned1)):
        for copy in copies:
            copy.wait_recv()
        attended_out[lead] = returned[lead, :, 0, :]
    store_cell.wait()
    store_hidden.wait()
    for copy in sends:
        copy.wait_send()


def picker(cols, members):
    pick = np.zeros((32, POOL, cols), np.float32)
    for k in range(members):
        pick[k, :, k * POOL : (k + 1) * POOL] = 1.0 / (POOL * POOL)
    for r in range(POOL):
        pick[16 + r, r, 0] = 1.0
        pick[24 + r, r, cols - 1] = 1.0
    return pick.reshape(32, POOL * cols)


def spreader(cols):
    spread = np.zeros((8, 128, 2, cols), np.float32)
    for pair in range(8):
        for j in range(2):
            r = 2 * pair + j
            for twin in (0, 32):
                spread[pair, twin + r, j, 0] = 1.0
                spread[pair, twin + 16 + r, j, cols - 1] = 1.0
    spread[:, 64:67] = 1.0
    return spread.reshape(8, 128, 2 * cols)


def body(
    frames,
    hidden_state,
    cell_state,
    depth_kernel,
    point_weight,
    gate_bias,
    mixing_weight,
    query_gain,
    output_weight,
):
    channels, row_count, cols = hidden_state.shape
    both = 2 * channels
    flat = channels * row_count
    n_rows, n_cols = lax.axis_size("rows"), lax.axis_size("cols")
    members = cols // POOL
    groups = n_rows // members
    any_space = pl.BlockSpec(memory_space=pl.ANY)
    vmem = pl.BlockSpec(memory_space=pltpu.VMEM)
    dma = pltpu.SemaphoreType.DMA
    hidden, cell, attended = pl.pallas_call(
        functools.partial(kernel, n_rows, n_cols, groups, members),
        out_shape=(
            jax.ShapeDtypeStruct((flat, cols), BF16),
            jax.ShapeDtypeStruct((flat, cols), F32),
            jax.ShapeDtypeStruct((LEADS, members, both), F32),
        ),
        in_specs=[any_space] * 4 + [vmem] * 7,
        out_specs=(any_space, any_space, vmem),
        scratch_shapes=[
            pltpu.VMEM((LEADS, flat, cols), BF16),
            pltpu.VMEM((flat, cols), BF16),
            pltpu.VMEM((flat, cols), F32),
            pltpu.VMEM((flat, cols), F32),
            pltpu.VMEM((row_count + 2, both, cols), F32),
            pltpu.VMEM((row_count + 2, both, cols), F32),
            pltpu.VMEM((9, both, cols), F32),
            pltpu.VMEM((8, 2 * both, 2 * cols), BF16),
            pltpu.VMEM((8, 2 * both, 2 * cols), BF16),
            pltpu.VMEM((4 * channels, 2 * both), BF16),
            pltpu.VMEM((both, POOL * cols), BF16),
            pltpu.VMEM((2, 3 * channels, cols), BF16),
            pltpu.VMEM((2, 3 * channels, cols), BF16),
            pltpu.VMEM((3, 16, both), BF16),
            pltpu.VMEM((6, 3, 16, both), BF16),
            pltpu.VMEM((2, channels, cols), BF16),
            pltpu.VMEM((2, channels, cols), BF16),
            pltpu.VMEM((16, both), BF16),
            pltpu.VMEM((6, 16, both), BF16),
            pltpu.VMEM((32, both), F32),
            pltpu.VMEM((3, both, both), BF16),
            pltpu.VMEM((both, both), BF16),
            pltpu.VMEM((LEADS, members, 1, both), F32),
            pltpu.VMEM((LEADS, members, 1, both), F32),
            pltpu.VMEM((LEADS, groups, members, both), BF16),
            pltpu.VMEM((LEADS, members, 1, both), F32),
            pltpu.VMEM((LEADS, members, 1, both), F32),
            dma((8,)),
            dma((2, 2)),
            dma((2, 2)),
            dma((2, 6)),
            dma((2, 6)),
            dma((LEADS, members)),
            dma((LEADS, members)),
            dma((LEADS, groups)),
            dma((LEADS, groups)),
            dma((LEADS, members)),
            dma((LEADS, members)),
        ],
        compiler_params=pltpu.CompilerParams(
            collective_id=0, has_side_effects=True, vmem_limit_bytes=40 * 2**20
        ),
    )(
        frames.reshape(LEADS, flat, cols),
        hidden_state.reshape(flat, cols),
        cell_state.reshape(flat, cols),
        jnp.asarray(spreader(cols), BF16),
        jnp.asarray(picker(cols, members), BF16),
        depth_kernel.reshape(both, 9),
        point_weight,
        gate_bias[None],
        mixing_weight,
        query_gain[None],
        output_weight,
    )
    attended = jnp.transpose(attended.reshape(LEADS, members, 2, channels), (0, 3, 2, 1))
    shape = (channels, row_count, cols)
    return (hidden.reshape(shape), cell.reshape(shape), attended)


def solution(mesh):
    in_specs = (
        P(None, None, "rows", "cols"),
        P(None, "rows", "cols"),
        P(None, "rows", "cols"),
        P(),
        P(),
        P(),
        P(),
        P(),
        P(),
    )
    out_specs = (P(None, "rows", "cols"), P(None, "rows", "cols"), P(None, None, "rows", "cols"))
    return jax.shard_map(body, mesh=mesh, in_specs=in_specs, out_specs=out_specs, check_vma=False)
```

```python
import functools
import math

import jax
import jax.numpy as jnp
import numpy as np
from jax import lax
from jax.experimental import pallas as pl
from jax.experimental.pallas import tpu as pltpu
from jax.sharding import PartitionSpec as P

LEADS = 2
POOL = 8
LINES = 4
MESH = pl.DeviceIdType.MESH
F32 = jnp.float32
BF16 = jnp.bfloat16
ROW_WAYS = (-1, 1)
EDGE_WAYS = tuple((dr, dc) for dr in (-1, 0, 1) for dc in (-1, 1))


def dot(left, right):
    return jnp.dot(left, right, preferred_element_type=F32)


def dot_t(left, right):
    return lax.dot_general(left, right, (((1,), (1,)), ((), ())), preferred_element_type=F32)


def lane_half(shape):
    return lax.broadcasted_iota(jnp.int32, shape, len(shape) - 1) < shape[-1] // 2


def half_norm(vectors, low):
    squares = vectors * vectors
    count = vectors.shape[-1] // 2
    first = jnp.sum(jnp.where(low, squares, 0.0), axis=-1, keepdims=True) / count
    second = jnp.sum(jnp.where(low, 0.0, squares), axis=-1, keepdims=True) / count
    return vectors * jnp.where(low, lax.rsqrt(first + 1e-06), lax.rsqrt(second + 1e-06))


def twice(weight):
    wide = jnp.concatenate([weight, weight], axis=1)
    low = lane_half(wide.shape)
    return jnp.concatenate([jnp.where(low, wide, 0.0), jnp.where(low, 0.0, wide)], axis=0)


def attend_column(own, every, mix_ref, gain, out_weight):
    lanes = own.shape[-1]
    low = lane_half(own.shape)
    queries = half_norm(dot_t(own, mix_ref[0]), low) * gain
    turned = pltpu.roll(queries, lanes // 2, 1)
    stacked = jnp.concatenate(
        [
            jnp.where(low, queries, 0.0),
            jnp.where(low, turned, 0.0),
            jnp.where(low, 0.0, turned),
            jnp.where(low, 0.0, queries),
        ],
        axis=0,
    ).astype(BF16)
    keys = half_norm(dot_t(every, mix_ref[1]), lane_half(every.shape)).astype(BF16)
    values = dot_t(every, mix_ref[2]).astype(BF16)
    scores = dot_t(stacked, keys) * (1.0 / math.sqrt(lanes // 2))
    count = own.shape[0]
    query_column = lax.broadcasted_iota(jnp.int32, scores.shape, 0) // 8 % 2
    key_column = lax.broadcasted_iota(jnp.int32, scores.shape, 1) // 8 % 2
    scores = jnp.where(query_column == key_column, scores, -1e30)
    highest = jnp.max(scores, axis=1, keepdims=True)
    highest = jnp.maximum(highest[: 2 * count], highest[2 * count :])
    weights = jnp.exp(scores - jnp.concatenate([highest, highest], axis=0))
    mass = jnp.sum(weights, axis=1, keepdims=True)
    mass = mass[: 2 * count] + mass[2 * count :]
    weighted = dot(weights.astype(BF16), values)
    swapped = pltpu.roll(weighted, lanes // 2, 1)
    mixed = jnp.where(
        low,
        (weighted[:count] + swapped[2 * count : 3 * count]) / mass[:count],
        (swapped[count : 2 * count] + weighted[3 * count :]) / mass[count:],
    )
    return own.astype(F32) + dot_t(mixed.astype(BF16), out_weight)


def depthwise(x_ref, taps_ref, spatial_ref, blocks, bands):
    cols = x_ref.shape[2]

    def block(index, carry):
        lo = pl.multiple_of(index * 16, 16)
        taps = [taps_ref[k, pl.ds(lo, 16), :][None] for k in range(9)]
        for start, count in bands:
            rows = x_ref[start : start + count + 2, pl.ds(lo, 16), :]
            left, middle, right = (
                taps[b] * rows[:count]
                + taps[3 + b] * rows[1 : count + 1]
                + taps[6 + b] * rows[2 : count + 2]
                for b in range(3)
            )
            lane = lax.broadcasted_iota(jnp.int32, (count * 16, cols), 1)
            left = pltpu.roll(left.reshape(count * 16, cols), 1, 1)
            right = pltpu.roll(right.reshape(count * 16, cols), cols - 1, 1)
            total = (
                jnp.where(lane == 0, 0.0, left)
                + middle.reshape(count * 16, cols)
                + jnp.where(lane == cols - 1, 0.0, right)
            ).astype(BF16)
            for j in range(count):
                row = start + j
                spatial_ref[row // 2, pl.ds(lo, 16), (row % 2) * cols : (row % 2 + 1) * cols] = (
                    total[j * 16 : (j + 1) * 16]
                )
        return carry

    lax.fori_loop(blocks[0], blocks[1], block, None)


def halo_column(frame_tiles, hidden_tiles, way, masks, taps_t, pad_ref):
    seen, above, below = masks
    first = 8 if way == 1 else 0
    slot = {dr: EDGE_WAYS.index((dr, way)) for dr in (-1, 0, 1)}

    def part(dr):
        frame = frame_tiles(slot[dr]).astype(F32)[first : first + 8]
        hidden = hidden_tiles(slot[dr]).astype(F32)[first : first + 8]
        low = lane_half(frame.shape)
        half = frame.shape[1] // 2
        upper = jnp.where(low, frame, pltpu.roll(hidden, half, 1))
        lower = jnp.where(low, pltpu.roll(frame, half, 1), hidden)
        return jnp.where(seen, upper, 0.0), jnp.where(seen, lower, 0.0)

    upper, lower = part(0)
    pad_ref[0:8] = jnp.where(above, part(1)[1], 0.0)
    pad_ref[8:16] = upper
    pad_ref[16:24] = lower
    pad_ref[24:32] = jnp.where(below, part(-1)[0], 0.0)
    b = 0 if way == 1 else 2
    return sum(taps_t[3 * a + b] * pad_ref[7 + a : 23 + a] for a in range(3))


def kernel(
    n_rows,
    n_cols,
    groups,
    members,
    frames_ref,
    hidden_ref,
    cell_ref,
    spread_ref,
    pick_ref,
    depth_ref,
    point_ref,
    bias_ref,
    mixing_ref,
    gain_ref,
    output_ref,
    hidden_out,
    cell_out,
    attended_out,
    point_in,
    depth_in,
    bias_in,
    mixing_in,
    gain_in,
    output_in,
    pick_in,
    frames_in,
    hidden_in,
    cell_now,
    plain,
    x0,
    x1,
    taps,
    spatial0,
    spatial1,
    weight,
    stacked,
    row_out0,
    row_in0,
    edge_out0,
    edge_in0,
    row_out1,
    row_in1,
    edge_out1,
    edge_in1,
    pad,
    mix,
    out_mix,
    given,
    column,
    gathered,
    result,
    returned,
    local_sem,
    send_row,
    recv_row,
    send_edge,
    recv_edge,
    send_a,
    recv_a,
    send_b,
    recv_b,
    send_c,
    recv_c,
):
    row, col = lax.axis_index("rows"), lax.axis_index("cols")
    core, group, line = row % 2, row // 2 % groups, row // (2 * groups)
    member = line * 2 + core
    channels = hidden_in.shape[0] // 16
    both = 2 * channels
    cols = hidden_in.shape[1]

    def near(dr, dc):
        return ((row + dr + n_rows) % n_rows, (col + dc + n_cols) % n_cols)

    def mate(step):
        target = (member + step) % members
        return ((target // 2 * groups + group) * 2 + target % 2, col)

    def twin(step):
        return ((line * groups + (group + step) % groups) * 2 + core, col)

    loads = [
        pltpu.make_async_copy(frames_ref.at[0], frames_in.at[0], local_sem.at[0]),
        pltpu.make_async_copy(hidden_ref, hidden_in, local_sem.at[1]),
        pltpu.make_async_copy(frames_ref.at[1], frames_in.at[1], local_sem.at[2]),
        pltpu.make_async_copy(cell_ref, cell_now, local_sem.at[3]),
        pltpu.make_async_copy(spread_ref, spatial0.at[:, both:], local_sem.at[4]),
        pltpu.make_async_copy(spread_ref, spatial1.at[:, both:], local_sem.at[5]),
    ]
    small = [
        pltpu.make_async_copy(source, target, local_sem.at[8 + k])
        for k, (source, target) in enumerate(
            (
                (pick_ref, pick_in),
                (depth_ref, depth_in),
                (point_ref, point_in),
                (bias_ref, bias_in),
                (mixing_ref, mixing_in),
                (gain_ref, gain_in),
                (output_ref, output_in),
            )
        )
    ]
    for load in loads[:1] + small[:1] + loads[1:] + small[1:]:
        load.start()

    barrier = pltpu.get_barrier_semaphore()
    peers = [near(dr, dc) for dr, dc in EDGE_WAYS] + [near(dr, 0) for dr in ROW_WAYS]
    peers += [twin(step) for step in range(1, groups)] + [mate(step) for step in range(1, members)]
    for peer in peers:
        pl.semaphore_signal(barrier, inc=1, device_id=peer, device_id_type=MESH)

    small[0].wait()
    pick_edges = pick_in[16:, :]
    for k, (source, load) in enumerate(
        ((frames_in.at[0], loads[0]), (hidden_in, loads[1]), (frames_in.at[1], loads[2]))
    ):
        load.wait()
        plain[...] = source[...].astype(F32)
        target, base = ((x0, 0), (x0, channels), (x1, 0))[k]
        for r in range(16):
            plane = plain[pl.ds(r, channels, stride=16), :]
            target[r + 1, base : base + channels, :] = plane
            low = plane.astype(BF16)
            stacked[
                (r // 8) * channels : (r // 8 + 1) * channels, (r % 8) * cols : (r % 8 + 1) * cols
            ] = low
            if r in (0, 15):
                row_out0[r // 15, k * channels : (k + 1) * channels, :] = low
        edge_out0[k] = dot_t(pick_edges, stacked[...]).astype(BF16)

    pl.semaphore_wait(barrier, len(peers))
    sends = []

    def send(source, target, send_sem, recv_sem, device):
        copy = pltpu.make_async_remote_copy(
            src_ref=source,
            dst_ref=target,
            send_sem=send_sem,
            recv_sem=recv_sem,
            device_id=device,
            device_id_type=MESH,
        )
        copy.start()
        sends.append(copy)
        return copy

    def send_halo(step, row_out, row_in, edge_out, edge_in):
        copies = []
        for k, dr in enumerate(ROW_WAYS):
            copies.append(
                send(
                    row_out.at[k],
                    row_in.at[k],
                    send_row.at[step, k],
                    recv_row.at[step, k],
                    near(dr, 0),
                )
            )
        for k, (dr, dc) in enumerate(EDGE_WAYS):
            copies.append(
                send(
                    edge_out,
                    edge_in.at[k],
                    send_edge.at[step, k],
                    recv_edge.at[step, k],
                    near(dr, dc),
                )
            )
        return copies

    halo0 = send_halo(0, row_out0, row_in0, edge_out0, edge_in0)

    for load in small[1:]:
        load.wait()
    taps_t = [depth_in[k // 3, k % 3 : k % 3 + 1, :] for k in range(9)]
    depth = jnp.transpose(jnp.concatenate(taps_t + [jnp.zeros((both - 9, both), F32)], axis=0))
    for k in range(9):
        taps[k] = jnp.broadcast_to(depth[:, k : k + 1], (both, cols))
    lane = lax.broadcasted_iota(jnp.int32, (4 * channels, cols), 1)
    sublane = lax.broadcasted_iota(jnp.int32, (4 * channels, cols), 0)
    halve = jnp.where(sublane < 3 * channels, 0.5, 1.0)
    bias = jnp.transpose(jnp.broadcast_to(bias_in[...], (cols, 4 * channels))) * halve
    weight[:, :both] = (point_in[...].astype(F32) * halve).astype(BF16)
    for part in range(3):
        rounded = bias.astype(BF16).astype(F32)
        bias_lanes = rounded if part == 0 else jnp.where(lane == 64 + part, rounded, bias_lanes)
        bias = bias - rounded
    bias_lanes = jnp.where(lane < 67, bias_lanes, 0.0)
    mixing = jnp.transpose(mixing_in[...].astype(F32))
    for k in range(3):
        mix[k] = twice(mixing[k * channels : (k + 1) * channels]).astype(BF16)
    out_mix[...] = twice(output_in[...].astype(F32)).astype(BF16)
    gain = jnp.concatenate([gain_in[...], gain_in[...]], axis=1)

    above, below = row > 0, row < n_rows - 1
    interior, rim = ((1, 4), (5, 4), (9, 4), (13, 2)), ((0, 1), (15, 1))
    whole = channels // 16
    depthwise(x0, taps, spatial0, (0, 2 * whole), interior)
    depthwise(x1, taps, spatial1, (0, whole), interior)

    def fill_rows(x_ref, base, row_in, offset):
        x_ref[0, base : base + channels, :] = jnp.where(
            above, row_in[1, offset : offset + channels, :].astype(F32), 0.0
        )
        x_ref[17, base : base + channels, :] = jnp.where(
            below, row_in[0, offset : offset + channels, :].astype(F32), 0.0
        )

    def extend(frame_tiles, hidden_tiles):
        left = halo_column(frame_tiles, hidden_tiles, 1, (col > 0, above, below), taps_t, pad)
        right = halo_column(
            frame_tiles, hidden_tiles, -1, (col < n_cols - 1, above, below), taps_t, pad
        )
        rest = jnp.zeros((cols - 64, both), F32)
        added = jnp.concatenate([left, right, left, right, rest], axis=0).astype(BF16)
        lifted = dot_t(weight[:, :both], added)
        rounded = lifted.astype(BF16).astype(F32)
        weight[:, both:] = jnp.where(
            lane < 32, rounded, jnp.where(lane < 64, lifted - rounded, bias_lanes)
        ).astype(BF16)

    def update(step, spatial):
        for pair in range(8):
            gates = dot(weight[...], spatial[pair])
            for j in range(2):
                r = 2 * pair + j
                in_gate, forget, out_gate, candidate = (
                    jnp.tanh(gates[k * channels : (k + 1) * channels, j * cols : (j + 1) * cols])
                    for k in range(4)
                )
                place = pl.ds(r, channels, stride=16)
                memory = (0.5 * forget + 0.5) * cell_now[place, :] + (
                    0.5 * in_gate + 0.5
                ) * candidate
                cell_now[place, :] = memory
                hidden = (0.5 * out_gate + 0.5) * jnp.tanh(memory)
                low = hidden.astype(BF16)
                stacked[
                    (r // 8) * channels : (r // 8 + 1) * channels,
                    (r % 8) * cols : (r % 8 + 1) * cols,
                ] = low
                if step == 0:
                    x1[r + 1, channels:both, :] = low.astype(F32)
                    if r in (0, 15):
                        row_out1[r // 15] = low
                else:
                    plain[place, :] = hidden

    def share(lead, pooled):
        pooled = pooled.astype(BF16).astype(F32)
        for k in range(members):
            given[lead, k] = pooled[2 * k : 2 * k + 2]
        column[lead, member] = given[lead, member]
        copies = []
        for step in range(1, members):
            copies.append(
                send(
                    given.at[lead, (member + step) % members],
                    column.at[lead, member],
                    send_a.at[lead, step],
                    recv_a.at[lead, step],
                    mate(step),
                )
            )
        return copies

    def gather(lead, copies):
        for copy in copies:
            copy.wait_recv()
        gathered[lead, group] = jnp.concatenate(
            [column[lead, :, k, :] for k in range(2)], axis=0
        ).astype(BF16)
        copies = []
        for step in range(1, groups):
            copies.append(
                send(
                    gathered.at[lead, group],
                    gathered.at[lead, group],
                    send_b.at[lead, step],
                    recv_b.at[lead, step],
                    twin(step),
                )
            )
        return copies

    def attend(lead, copies):
        for copy in copies:
            copy.wait_recv()
        attended = attend_column(
            gathered[lead, group],
            gathered[lead].reshape(groups * 2 * members, both),
            mix,
            gain,
            out_mix[...],
        )
        for k in range(2):
            result[lead, :, k, :] = attended[k * members : (k + 1) * members]
        returned[lead, member] = result[lead, member]
        copies = []
        for step in range(1, members):
            copies.append(
                send(
                    result.at[lead, (member + step) % members],
                    returned.at[lead, member],
                    send_c.at[lead, step],
                    recv_c.at[lead, step],
                    mate(step),
                )
            )
        return copies

    for copy in halo0:
        copy.wait_recv()
    fill_rows(x0, 0, row_in0, 0)
    fill_rows(x0, channels, row_in0, channels)
    depthwise(x0, taps, spatial0, (0, 2 * whole), rim)
    extend(lambda k: edge_in0[k, 0], lambda k: edge_in0[k, 1])
    for load in loads[3:]:
        load.wait()
    update(0, spatial0)
    picked = dot_t(pick_in[...], stacked[...])
    edge_out1[...] = picked[16:].astype(BF16)
    halo1 = send_halo(1, row_out1, row_in1, edge_out1, edge_in1)
    shared0 = share(0, picked[:16])
    fill_rows(x1, 0, row_in0, both)
    depthwise(x1, taps, spatial1, (0, whole), rim)
    depthwise(x1, taps, spatial1, (whole, 2 * whole), interior)
    for copy in halo1:
        copy.wait_recv()
    fill_rows(x1, channels, row_in1, 0)
    depthwise(x1, taps, spatial1, (whole, 2 * whole), rim)
    extend(lambda k: edge_in0[k, 2], lambda k: edge_in1[k])
    gathered0 = gather(0, shared0)
    update(1, spatial1)
    picked = dot_t(pick_in[:16, :], stacked[...])
    shared1 = share(1, picked)
    store_cell = pltpu.make_async_copy(cell_now, cell_out, local_sem.at[6])
    store_cell.start()
    hidden_in[...] = plain[...].astype(BF16)
    store_hidden = pltpu.make_async_copy(hidden_in, hidden_out, local_sem.at[7])
    store_hidden.start()
    returned0 = attend(0, gathered0)
    gathered1 = gather(1, shared1)
    returned1 = attend(1, gathered1)
    for lead, copies in enumerate((returned0, returned1)):
        for copy in copies:
            copy.wait_recv()
        attended = jnp.concatenate([returned[lead, k] for k in range(members)], axis=0)
        for k in range(2):
            attended_out[lead, k] = attended[:, k * channels : (k + 1) * channels]
    store_cell.wait()
    store_hidden.wait()
    for copy in sends:
        copy.wait_send()


def picker(cols):
    pick = np.zeros((32, POOL, cols), np.float32)
    for k in range(cols // POOL):
        pick[k, :, k * POOL : (k + 1) * POOL] = 1.0 / (POOL * POOL)
    for r in range(POOL):
        pick[16 + r, r, 0] = 1.0
        pick[24 + r, r, cols - 1] = 1.0
    return pick.reshape(32, POOL * cols)


def spreader(cols):
    spread = np.zeros((8, 128, 2, cols), np.float32)
    for pair in range(8):
        for j in range(2):
            r = 2 * pair + j
            for twin in (0, 32):
                spread[pair, twin + r, j, 0] = 1.0
                spread[pair, twin + 16 + r, j, cols - 1] = 1.0
    spread[:, 64:67] = 1.0
    return spread.reshape(8, 128, 2 * cols)


def body(
    frames,
    hidden_state,
    cell_state,
    depth_kernel,
    point_weight,
    gate_bias,
    mixing_weight,
    query_gain,
    output_weight,
):
    channels, row_count, cols = hidden_state.shape
    both = 2 * channels
    flat = channels * row_count
    n_rows, n_cols = lax.axis_size("rows"), lax.axis_size("cols")
    members = 2 * LINES
    groups = n_rows // members
    hbm = pl.BlockSpec(memory_space=pltpu.HBM)
    any_space = pl.BlockSpec(memory_space=pl.ANY)
    vmem = pl.BlockSpec(memory_space=pltpu.VMEM)
    dma = pltpu.SemaphoreType.DMA
    hidden, cell, attended = pl.pallas_call(
        functools.partial(kernel, n_rows, n_cols, groups, members),
        out_shape=(
            jax.ShapeDtypeStruct((flat, cols), BF16),
            jax.ShapeDtypeStruct((flat, cols), F32),
            jax.ShapeDtypeStruct((LEADS, 2, cols // POOL, channels), F32),
        ),
        in_specs=[hbm] * 11,
        out_specs=(any_space, any_space, vmem),
        scratch_shapes=[
            pltpu.VMEM((4 * channels, both), BF16),
            pltpu.VMEM((3, 3, both), F32),
            pltpu.VMEM((1, 4 * channels), F32),
            pltpu.VMEM((channels, 3 * channels), BF16),
            pltpu.VMEM((1, channels), F32),
            pltpu.VMEM((channels, channels), BF16),
            pltpu.VMEM((32, POOL * cols), BF16),
            pltpu.VMEM((LEADS, flat, cols), BF16),
            pltpu.VMEM((flat, cols), BF16),
            pltpu.VMEM((flat, cols), F32),
            pltpu.VMEM((flat, cols), F32),
            pltpu.VMEM((row_count + 2, both, cols), F32),
            pltpu.VMEM((row_count + 2, both, cols), F32),
            pltpu.VMEM((9, both, cols), F32),
            pltpu.VMEM((8, 2 * both, 2 * cols), BF16),
            pltpu.VMEM((8, 2 * both, 2 * cols), BF16),
            pltpu.VMEM((4 * channels, 2 * both), BF16),
            pltpu.VMEM((both, POOL * cols), BF16),
            pltpu.VMEM((2, 3 * channels, cols), BF16),
            pltpu.VMEM((2, 3 * channels, cols), BF16),
            pltpu.VMEM((3, 16, both), BF16),
            pltpu.VMEM((6, 3, 16, both), BF16),
            pltpu.VMEM((2, channels, cols), BF16),
            pltpu.VMEM((2, channels, cols), BF16),
            pltpu.VMEM((16, both), BF16),
            pltpu.VMEM((6, 16, both), BF16),
            pltpu.VMEM((32, both), F32),
            pltpu.VMEM((3, both, both), BF16),
            pltpu.VMEM((both, both), BF16),
            pltpu.VMEM((LEADS, members, 2, both), F32),
            pltpu.VMEM((LEADS, members, 2, both), F32),
            pltpu.VMEM((LEADS, groups, 2 * members, both), BF16),
            pltpu.VMEM((LEADS, members, 2, both), F32),
            pltpu.VMEM((LEADS, members, 2, both), F32),
            dma((15,)),
            dma((2, 2)),
            dma((2, 2)),
            dma((2, 6)),
            dma((2, 6)),
            dma((LEADS, members)),
            dma((LEADS, members)),
            dma((LEADS, groups)),
            dma((LEADS, groups)),
            dma((LEADS, members)),
            dma((LEADS, members)),
        ],
        compiler_params=pltpu.CompilerParams(
            collective_id=0, has_side_effects=True, vmem_limit_bytes=60 * 2**20
        ),
    )(
        frames.reshape(LEADS, flat, cols),
        hidden_state.reshape(flat, cols),
        cell_state.reshape(flat, cols),
        jnp.asarray(spreader(cols), BF16),
        jnp.asarray(picker(cols), BF16),
        jnp.transpose(depth_kernel, (1, 2, 0)),
        point_weight,
        gate_bias[None],
        mixing_weight.T,
        query_gain[None],
        output_weight,
    )
    attended = jnp.transpose(attended, (0, 3, 1, 2))
    shape = (channels, row_count, cols)
    return (hidden.reshape(shape), cell.reshape(shape), attended)


def solution(mesh):
    in_specs = (
        P(None, None, "rows", "cols"),
        P(None, "rows", "cols"),
        P(None, "rows", "cols"),
        P(),
        P(),
        P(),
        P(),
        P(),
        P(),
    )
    out_specs = (P(None, "rows", "cols"), P(None, "rows", "cols"), P(None, None, "rows", "cols"))
    return jax.shard_map(body, mesh=mesh, in_specs=in_specs, out_specs=out_specs, check_vma=False)
```

```python
import functools
import math

import jax
import jax.numpy as jnp
import numpy as np
from jax import lax
from jax.experimental import pallas as pl
from jax.experimental.pallas import tpu as pltpu
from jax.sharding import PartitionSpec as P

LEADS = 2
POOL = 8
LINES = 4
DEEP = 3
MESH = pl.DeviceIdType.MESH
F32 = jnp.float32
BF16 = jnp.bfloat16
ROW_WAYS = (-1, 1)
EDGE_WAYS = tuple((dr, dc) for dr in (-1, 0, 1) for dc in (-1, 1))


def dot(left, right):
    return jnp.dot(left, right, preferred_element_type=F32)


def dot_t(left, right):
    return lax.dot_general(left, right, (((1,), (1,)), ((), ())), preferred_element_type=F32)


def lane_half(shape):
    return lax.broadcasted_iota(jnp.int32, shape, len(shape) - 1) < shape[-1] // 2


def half_norm(vectors, low):
    squares = vectors * vectors
    count = vectors.shape[-1] // 2
    first = jnp.sum(jnp.where(low, squares, 0.0), axis=-1, keepdims=True) / count
    second = jnp.sum(jnp.where(low, 0.0, squares), axis=-1, keepdims=True) / count
    return vectors * jnp.where(low, lax.rsqrt(first + 1e-06), lax.rsqrt(second + 1e-06))


def twice(weight):
    wide = jnp.concatenate([weight, weight], axis=1)
    low = lane_half(wide.shape)
    return jnp.concatenate([jnp.where(low, wide, 0.0), jnp.where(low, 0.0, wide)], axis=0)


def attend_column(own, every, mix_ref, gain, out_weight):
    lanes = own.shape[-1]
    low = lane_half(own.shape)
    queries = half_norm(dot_t(own, mix_ref[0]), low) * gain
    turned = pltpu.roll(queries, lanes // 2, 1)
    stacked = jnp.concatenate(
        [
            jnp.where(low, queries, 0.0),
            jnp.where(low, turned, 0.0),
            jnp.where(low, 0.0, turned),
            jnp.where(low, 0.0, queries),
        ],
        axis=0,
    ).astype(BF16)
    keys = half_norm(dot_t(every, mix_ref[1]), lane_half(every.shape)).astype(BF16)
    values = dot_t(every, mix_ref[2]).astype(BF16)
    scores = dot_t(stacked, keys) * (1.0 / math.sqrt(lanes // 2))
    count = own.shape[0]
    query_column = lax.broadcasted_iota(jnp.int32, scores.shape, 0) // 8 % 2
    key_column = lax.broadcasted_iota(jnp.int32, scores.shape, 1) // 8 % 2
    scores = jnp.where(query_column == key_column, scores, -1e30)
    highest = jnp.max(scores, axis=1, keepdims=True)
    highest = jnp.maximum(highest[: 2 * count], highest[2 * count :])
    weights = jnp.exp(scores - jnp.concatenate([highest, highest], axis=0))
    mass = jnp.sum(weights, axis=1, keepdims=True)
    mass = mass[: 2 * count] + mass[2 * count :]
    weighted = dot(weights.astype(BF16), values)
    swapped = pltpu.roll(weighted, lanes // 2, 1)
    mixed = jnp.where(
        low,
        (weighted[:count] + swapped[2 * count : 3 * count]) / mass[:count],
        (swapped[count : 2 * count] + weighted[3 * count :]) / mass[count:],
    )
    return own.astype(F32) + dot_t(mixed.astype(BF16), out_weight)


def depthwise(x_ref, taps_ref, spatial_ref, blocks, bands):
    cols = x_ref.shape[2]

    def block(index, carry):
        lo = pl.multiple_of(index * 16, 16)
        taps = [taps_ref[k, pl.ds(lo, 16), :][None] for k in range(9)]
        for start, count in bands:
            rows = x_ref[start : start + count + 2, pl.ds(lo, 16), :]
            left, middle, right = (
                taps[b] * rows[:count]
                + taps[3 + b] * rows[1 : count + 1]
                + taps[6 + b] * rows[2 : count + 2]
                for b in range(3)
            )
            lane = lax.broadcasted_iota(jnp.int32, (count * 16, cols), 1)
            left = pltpu.roll(left.reshape(count * 16, cols), 1, 1)
            right = pltpu.roll(right.reshape(count * 16, cols), cols - 1, 1)
            total = (
                jnp.where(lane == 0, 0.0, left)
                + middle.reshape(count * 16, cols)
                + jnp.where(lane == cols - 1, 0.0, right)
            ).astype(BF16)
            for j in range(count):
                row = start + j
                spatial_ref[row // 2, pl.ds(lo, 16), (row % 2) * cols : (row % 2 + 1) * cols] = (
                    total[j * 16 : (j + 1) * 16]
                )
        return carry

    lax.fori_loop(blocks[0], blocks[1], block, None)


def halo_column(frame_tiles, hidden_tiles, way, masks, taps_t, pad_ref):
    seen, above, below = masks
    first = 8 if way == 1 else 0
    slot = {dr: EDGE_WAYS.index((dr, way)) for dr in (-1, 0, 1)}

    def part(dr):
        frame = frame_tiles(slot[dr]).astype(F32)[first : first + 8]
        hidden = hidden_tiles(slot[dr]).astype(F32)[first : first + 8]
        low = lane_half(frame.shape)
        half = frame.shape[1] // 2
        upper = jnp.where(low, frame, pltpu.roll(hidden, half, 1))
        lower = jnp.where(low, pltpu.roll(frame, half, 1), hidden)
        return jnp.where(seen, upper, 0.0), jnp.where(seen, lower, 0.0)

    upper, lower = part(0)
    pad_ref[0:8] = jnp.where(above, part(1)[1], 0.0)
    pad_ref[8:16] = upper
    pad_ref[16:24] = lower
    pad_ref[24:32] = jnp.where(below, part(-1)[0], 0.0)
    b = 0 if way == 1 else 2
    return sum(taps_t[3 * a + b] * pad_ref[7 + a : 23 + a] for a in range(3))


def kernel(
    n_rows,
    n_cols,
    groups,
    members,
    frames_ref,
    hidden_ref,
    cell_ref,
    spread_ref,
    pick_ref,
    depth_ref,
    point_ref,
    bias_ref,
    mixing_ref,
    gain_ref,
    output_ref,
    hidden_out,
    cell_out,
    attended_out,
    point_in,
    depth_in,
    bias_in,
    mixing_in,
    gain_in,
    output_in,
    pick_in,
    frames_in,
    hidden_in,
    cell_now,
    plain,
    x0,
    x1,
    taps,
    spatial0,
    spatial1,
    weight,
    stacked,
    row_out0,
    row_in0,
    edge_out0,
    edge_in0,
    row_out1,
    row_in1,
    edge_out1,
    edge_in1,
    pad,
    mix,
    out_mix,
    given,
    column,
    gathered,
    result,
    returned,
    local_sem,
    send_row,
    recv_row,
    send_edge,
    recv_edge,
    send_a,
    recv_a,
    send_b,
    recv_b,
    send_c,
    recv_c,
    send_d,
    recv_d,
):
    row, col = lax.axis_index("rows"), lax.axis_index("cols")
    core, group, line = row % 2, row // 2 % groups, row // (2 * groups)
    member = line * 2 + core
    channels = hidden_in.shape[0] // 16
    both = 2 * channels
    cols = hidden_in.shape[1]

    def near(dr, dc):
        return ((row + dr + n_rows) % n_rows, (col + dc + n_cols) % n_cols)

    def mate(step):
        target = (member + step) % members
        return ((target // 2 * groups + group) * 2 + target % 2, col)

    span = groups // DEEP
    level, place_y = group // span, group % span

    def upper(step):
        return ((line * groups + (level + step) % DEEP * span + place_y) * 2 + core, col)

    def twin(step):
        return ((line * groups + level * span + (place_y + step) % span) * 2 + core, col)

    loads = [
        pltpu.make_async_copy(frames_ref.at[0], frames_in.at[0], local_sem.at[0]),
        pltpu.make_async_copy(hidden_ref, hidden_in, local_sem.at[1]),
        pltpu.make_async_copy(frames_ref.at[1], frames_in.at[1], local_sem.at[2]),
        pltpu.make_async_copy(cell_ref, cell_now, local_sem.at[3]),
        pltpu.make_async_copy(spread_ref, spatial0.at[:, both:], local_sem.at[4]),
        pltpu.make_async_copy(spread_ref, spatial1.at[:, both:], local_sem.at[5]),
    ]
    small = [
        pltpu.make_async_copy(source, target, local_sem.at[8 + k])
        for k, (source, target) in enumerate(
            (
                (pick_ref, pick_in),
                (depth_ref, depth_in),
                (point_ref, point_in),
                (bias_ref, bias_in),
                (mixing_ref, mixing_in),
                (gain_ref, gain_in),
                (output_ref, output_in),
            )
        )
    ]
    for load in loads[:1] + small[:1] + loads[1:] + small[1:]:
        load.start()

    barrier = pltpu.get_barrier_semaphore()
    peers = [near(dr, dc) for dr, dc in EDGE_WAYS] + [near(dr, 0) for dr in ROW_WAYS]
    peers += [upper(step) for step in range(1, DEEP)] + [twin(step) for step in range(1, span)]
    peers += [mate(step) for step in range(1, members)]
    for peer in peers:
        pl.semaphore_signal(barrier, inc=1, device_id=peer, device_id_type=MESH)

    small[0].wait()
    pick_edges = pick_in[16:, :]
    for k, (source, load) in enumerate(
        ((frames_in.at[0], loads[0]), (hidden_in, loads[1]), (frames_in.at[1], loads[2]))
    ):
        load.wait()
        plain[...] = source[...].astype(F32)
        target, base = ((x0, 0), (x0, channels), (x1, 0))[k]
        for r in range(16):
            plane = plain[pl.ds(r, channels, stride=16), :]
            target[r + 1, base : base + channels, :] = plane
            low = plane.astype(BF16)
            stacked[
                (r // 8) * channels : (r // 8 + 1) * channels, (r % 8) * cols : (r % 8 + 1) * cols
            ] = low
            if r in (0, 15):
                row_out0[r // 15, k * channels : (k + 1) * channels, :] = low
        edge_out0[k] = dot_t(pick_edges, stacked[...]).astype(BF16)

    pl.semaphore_wait(barrier, len(peers))
    sends = []

    def settle(keep):
        done = len(sends) - keep
        for copy in sends[:done]:
            copy.wait_send()
        del sends[:done]

    def send(source, target, send_sem, recv_sem, device):
        copy = pltpu.make_async_remote_copy(
            src_ref=source,
            dst_ref=target,
            send_sem=send_sem,
            recv_sem=recv_sem,
            device_id=device,
            device_id_type=MESH,
        )
        copy.start()
        sends.append(copy)
        return copy

    def send_halo(step, row_out, row_in, edge_out, edge_in):
        copies = []
        for k, dr in enumerate(ROW_WAYS):
            copies.append(
                send(
                    row_out.at[k],
                    row_in.at[k],
                    send_row.at[step, k],
                    recv_row.at[step, k],
                    near(dr, 0),
                )
            )
        for k, (dr, dc) in enumerate(EDGE_WAYS):
            copies.append(
                send(
                    edge_out,
                    edge_in.at[k],
                    send_edge.at[step, k],
                    recv_edge.at[step, k],
                    near(dr, dc),
                )
            )
        return copies

    halo0 = send_halo(0, row_out0, row_in0, edge_out0, edge_in0)

    for load in small[1:]:
        load.wait()
    taps_t = [depth_in[k // 3, k % 3 : k % 3 + 1, :] for k in range(9)]
    depth = jnp.transpose(jnp.concatenate(taps_t + [jnp.zeros((both - 9, both), F32)], axis=0))
    for k in range(9):
        taps[k] = jnp.broadcast_to(depth[:, k : k + 1], (both, cols))
    lane = lax.broadcasted_iota(jnp.int32, (4 * channels, cols), 1)
    sublane = lax.broadcasted_iota(jnp.int32, (4 * channels, cols), 0)
    halve = jnp.where(sublane < 3 * channels, 0.5, 1.0)
    bias = jnp.transpose(jnp.broadcast_to(bias_in[...], (cols, 4 * channels))) * halve
    weight[:, :both] = (point_in[...].astype(F32) * halve).astype(BF16)
    for part in range(3):
        rounded = bias.astype(BF16).astype(F32)
        bias_lanes = rounded if part == 0 else jnp.where(lane == 64 + part, rounded, bias_lanes)
        bias = bias - rounded
    bias_lanes = jnp.where(lane < 67, bias_lanes, 0.0)
    mixing = jnp.transpose(mixing_in[...].astype(F32))
    for k in range(3):
        mix[k] = twice(mixing[k * channels : (k + 1) * channels]).astype(BF16)
    out_mix[...] = twice(output_in[...].astype(F32)).astype(BF16)
    gain = jnp.concatenate([gain_in[...], gain_in[...]], axis=1)

    above, below = row > 0, row < n_rows - 1
    interior, rim = ((1, 4), (5, 4), (9, 4), (13, 2)), ((0, 1), (15, 1))
    whole = channels // 16
    depthwise(x0, taps, spatial0, (0, 2 * whole), interior)
    depthwise(x1, taps, spatial1, (0, whole), interior)

    def fill_rows(x_ref, base, row_in, offset):
        x_ref[0, base : base + channels, :] = jnp.where(
            above, row_in[1, offset : offset + channels, :].astype(F32), 0.0
        )
        x_ref[17, base : base + channels, :] = jnp.where(
            below, row_in[0, offset : offset + channels, :].astype(F32), 0.0
        )

    def extend(frame_tiles, hidden_tiles):
        left = halo_column(frame_tiles, hidden_tiles, 1, (col > 0, above, below), taps_t, pad)
        right = halo_column(
            frame_tiles, hidden_tiles, -1, (col < n_cols - 1, above, below), taps_t, pad
        )
        rest = jnp.zeros((cols - 64, both), F32)
        added = jnp.concatenate([left, right, left, right, rest], axis=0).astype(BF16)
        lifted = dot_t(weight[:, :both], added)
        rounded = lifted.astype(BF16).astype(F32)
        weight[:, both:] = jnp.where(
            lane < 32, rounded, jnp.where(lane < 64, lifted - rounded, bias_lanes)
        ).astype(BF16)

    def update(step, spatial):
        for pair in range(8):
            gates = dot(weight[...], spatial[pair])
            for j in range(2):
                r = 2 * pair + j
                in_gate, forget, out_gate, candidate = (
                    jnp.tanh(gates[k * channels : (k + 1) * channels, j * cols : (j + 1) * cols])
                    for k in range(4)
                )
                place = pl.ds(r, channels, stride=16)
                memory = (0.5 * forget + 0.5) * cell_now[place, :] + (
                    0.5 * in_gate + 0.5
                ) * candidate
                cell_now[place, :] = memory
                hidden = (0.5 * out_gate + 0.5) * jnp.tanh(memory)
                low = hidden.astype(BF16)
                stacked[
                    (r // 8) * channels : (r // 8 + 1) * channels,
                    (r % 8) * cols : (r % 8 + 1) * cols,
                ] = low
                if step == 0:
                    x1[r + 1, channels:both, :] = low.astype(F32)
                    if r in (0, 15):
                        row_out1[r // 15] = low
                else:
                    plain[place, :] = hidden

    def share(lead, pooled):
        pooled = pooled.astype(BF16).astype(F32)
        for k in range(members):
            given[lead, k] = pooled[2 * k : 2 * k + 2]
        column[lead, member] = given[lead, member]
        copies = []
        for step in range(1, members):
            copies.append(
                send(
                    given.at[lead, (member + step) % members],
                    column.at[lead, member],
                    send_a.at[lead, step],
                    recv_a.at[lead, step],
                    mate(step),
                )
            )
        return copies

    def gather(lead, copies):
        for copy in copies:
            copy.wait_recv()
        gathered[lead, place_y, level] = jnp.concatenate(
            [column[lead, :, k, :] for k in range(2)], axis=0
        ).astype(BF16)
        return [
            send(
                gathered.at[lead, place_y, level],
                gathered.at[lead, place_y, level],
                send_b.at[lead, step],
                recv_b.at[lead, step],
                upper(step),
            )
            for step in range(1, DEEP)
        ]

    def spread(lead, copies):
        for copy in copies:
            copy.wait_recv()
        return [
            send(
                gathered.at[lead, place_y],
                gathered.at[lead, place_y],
                send_d.at[lead, step],
                recv_d.at[lead, step],
                twin(step),
            )
            for step in range(1, span)
        ]

    def attend(lead, copies):
        for copy in copies:
            copy.wait_recv()
        attended = attend_column(
            gathered[lead, place_y, level],
            gathered[lead].reshape(groups * 2 * members, both),
            mix,
            gain,
            out_mix[...],
        )
        for k in range(2):
            result[lead, :, k, :] = attended[k * members : (k + 1) * members]
        returned[lead, member] = result[lead, member]
        copies = []
        for step in range(1, members):
            copies.append(
                send(
                    result.at[lead, (member + step) % members],
                    returned.at[lead, member],
                    send_c.at[lead, step],
                    recv_c.at[lead, step],
                    mate(step),
                )
            )
        return copies

    for copy in halo0:
        copy.wait_recv()
    fill_rows(x0, 0, row_in0, 0)
    fill_rows(x0, channels, row_in0, channels)
    depthwise(x0, taps, spatial0, (0, 2 * whole), rim)
    extend(lambda k: edge_in0[k, 0], lambda k: edge_in0[k, 1])
    for load in loads[3:]:
        load.wait()
    update(0, spatial0)
    picked = dot_t(pick_in[...], stacked[...])
    edge_out1[...] = picked[16:].astype(BF16)
    halo1 = send_halo(1, row_out1, row_in1, edge_out1, edge_in1)
    shared0 = share(0, picked[:16])
    fill_rows(x1, 0, row_in0, both)
    depthwise(x1, taps, spatial1, (0, whole), rim)
    depthwise(x1, taps, spatial1, (whole, 2 * whole), interior)
    for copy in halo1:
        copy.wait_recv()
    fill_rows(x1, channels, row_in1, 0)
    depthwise(x1, taps, spatial1, (whole, 2 * whole), rim)
    extend(lambda k: edge_in0[k, 2], lambda k: edge_in1[k])
    gathered0 = gather(0, shared0)
    update(1, spatial1)
    picked = dot_t(pick_in[:16, :], stacked[...])
    shared1 = share(1, picked)
    spread0 = spread(0, gathered0)
    settle(len(shared1) + len(spread0))
    store_cell = pltpu.make_async_copy(cell_now, cell_out, local_sem.at[6])
    store_cell.start()
    hidden_in[...] = plain[...].astype(BF16)
    store_hidden = pltpu.make_async_copy(hidden_in, hidden_out, local_sem.at[7])
    store_hidden.start()
    gathered1 = gather(1, shared1)
    returned0 = attend(0, spread0)
    spread1 = spread(1, gathered1)
    settle(len(spread1))
    returned1 = attend(1, spread1)
    for lead, copies in enumerate((returned0, returned1)):
        for copy in copies:
            copy.wait_recv()
        attended = jnp.concatenate([returned[lead, k] for k in range(members)], axis=0)
        for k in range(2):
            attended_out[lead, k] = attended[:, k * channels : (k + 1) * channels]
    store_cell.wait()
    store_hidden.wait()
    settle(0)


def finish_kernel(*refs):
    count = (len(refs) - 1) // 3
    sources, targets, held, sem = refs[:count], refs[count : 2 * count], refs[2 * count : -1], refs[-1]
    loads = [pltpu.make_async_copy(sources[k], held[k], sem.at[0, k]) for k in range(count)]
    stores = [pltpu.make_async_copy(held[k], targets[k], sem.at[1, k]) for k in range(count)]
    for load in loads:
        load.start()
    for load, store in zip(loads, stores):
        load.wait()
        store.start()
    for store in stores:
        store.wait()


def finish(*arrays):
    hbm = pl.BlockSpec(memory_space=pltpu.HBM)
    return pl.pallas_call(
        finish_kernel,
        out_shape=tuple(jax.ShapeDtypeStruct(a.shape, a.dtype) for a in arrays),
        in_specs=[hbm] * len(arrays),
        out_specs=(hbm,) * len(arrays),
        scratch_shapes=[pltpu.VMEM(a.shape, a.dtype) for a in arrays]
        + [pltpu.SemaphoreType.DMA((2, len(arrays)))],
        compiler_params=pltpu.CompilerParams(vmem_limit_bytes=60 * 2**20),
    )(*arrays)


def picker(cols):
    pick = np.zeros((32, POOL, cols), np.float32)
    for k in range(cols // POOL):
        pick[k, :, k * POOL : (k + 1) * POOL] = 1.0 / (POOL * POOL)
    for r in range(POOL):
        pick[16 + r, r, 0] = 1.0
        pick[24 + r, r, cols - 1] = 1.0
    return pick.reshape(32, POOL * cols)


def spreader(cols):
    spread = np.zeros((8, 128, 2, cols), np.float32)
    for pair in range(8):
        for j in range(2):
            r = 2 * pair + j
            for twin in (0, 32):
                spread[pair, twin + r, j, 0] = 1.0
                spread[pair, twin + 16 + r, j, cols - 1] = 1.0
    spread[:, 64:67] = 1.0
    return spread.reshape(8, 128, 2 * cols)


def body(
    frames,
    hidden_state,
    cell_state,
    depth_kernel,
    point_weight,
    gate_bias,
    mixing_weight,
    query_gain,
    output_weight,
):
    channels, row_count, cols = hidden_state.shape
    both = 2 * channels
    flat = channels * row_count
    n_rows, n_cols = lax.axis_size("rows"), lax.axis_size("cols")
    members = 2 * LINES
    groups = n_rows // members
    hbm = pl.BlockSpec(memory_space=pltpu.HBM)
    any_space = pl.BlockSpec(memory_space=pl.ANY)
    vmem = pl.BlockSpec(memory_space=pltpu.VMEM)
    dma = pltpu.SemaphoreType.DMA
    hidden, cell, attended = pl.pallas_call(
        functools.partial(kernel, n_rows, n_cols, groups, members),
        out_shape=(
            jax.ShapeDtypeStruct((flat, cols), BF16),
            jax.ShapeDtypeStruct((flat, cols), F32),
            jax.ShapeDtypeStruct((LEADS, 2, cols // POOL, channels), F32),
        ),
        in_specs=[hbm] * 11,
        out_specs=(any_space, any_space, vmem),
        scratch_shapes=[
            pltpu.VMEM((4 * channels, both), BF16),
            pltpu.VMEM((3, 3, both), F32),
            pltpu.VMEM((1, 4 * channels), F32),
            pltpu.VMEM((channels, 3 * channels), BF16),
            pltpu.VMEM((1, channels), F32),
            pltpu.VMEM((channels, channels), BF16),
            pltpu.VMEM((32, POOL * cols), BF16),
            pltpu.VMEM((LEADS, flat, cols), BF16),
            pltpu.VMEM((flat, cols), BF16),
            pltpu.VMEM((flat, cols), F32),
            pltpu.VMEM((flat, cols), F32),
            pltpu.VMEM((row_count + 2, both, cols), F32),
            pltpu.VMEM((row_count + 2, both, cols), F32),
            pltpu.VMEM((9, both, cols), F32),
            pltpu.VMEM((8, 2 * both, 2 * cols), BF16),
            pltpu.VMEM((8, 2 * both, 2 * cols), BF16),
            pltpu.VMEM((4 * channels, 2 * both), BF16),
            pltpu.VMEM((both, POOL * cols), BF16),
            pltpu.VMEM((2, 3 * channels, cols), BF16),
            pltpu.VMEM((2, 3 * channels, cols), BF16),
            pltpu.VMEM((3, 16, both), BF16),
            pltpu.VMEM((6, 3, 16, both), BF16),
            pltpu.VMEM((2, channels, cols), BF16),
            pltpu.VMEM((2, channels, cols), BF16),
            pltpu.VMEM((16, both), BF16),
            pltpu.VMEM((6, 16, both), BF16),
            pltpu.VMEM((32, both), F32),
            pltpu.VMEM((3, both, both), BF16),
            pltpu.VMEM((both, both), BF16),
            pltpu.VMEM((LEADS, members, 2, both), F32),
            pltpu.VMEM((LEADS, members, 2, both), F32),
            pltpu.VMEM((LEADS, groups // DEEP, DEEP, 2 * members, both), BF16),
            pltpu.VMEM((LEADS, members, 2, both), F32),
            pltpu.VMEM((LEADS, members, 2, both), F32),
            dma((15,)),
            dma((2, 2)),
            dma((2, 2)),
            dma((2, 6)),
            dma((2, 6)),
            dma((LEADS, members)),
            dma((LEADS, members)),
            dma((LEADS, DEEP)),
            dma((LEADS, DEEP)),
            dma((LEADS, members)),
            dma((LEADS, members)),
            dma((LEADS, groups // DEEP)),
            dma((LEADS, groups // DEEP)),
        ],
        compiler_params=pltpu.CompilerParams(
            collective_id=0, has_side_effects=True, vmem_limit_bytes=60 * 2**20
        ),
    )(
        frames.reshape(LEADS, flat, cols),
        hidden_state.reshape(flat, cols),
        cell_state.reshape(flat, cols),
        jnp.asarray(spreader(cols), BF16),
        jnp.asarray(picker(cols), BF16),
        jnp.transpose(depth_kernel, (1, 2, 0)),
        point_weight,
        gate_bias[None],
        mixing_weight.T,
        query_gain[None],
        output_weight,
    )
    attended, cell, hidden = finish(attended, cell, hidden)
    attended = jnp.transpose(attended, (0, 3, 1, 2))
    shape = (channels, row_count, cols)
    return (hidden.reshape(shape), cell.reshape(shape), attended)


def solution(mesh):
    in_specs = (
        P(None, None, "rows", "cols"),
        P(None, "rows", "cols"),
        P(None, "rows", "cols"),
        P(),
        P(),
        P(),
        P(),
        P(),
        P(),
    )
    out_specs = (P(None, "rows", "cols"), P(None, "rows", "cols"), P(None, None, "rows", "cols"))
    return jax.shard_map(body, mesh=mesh, in_specs=in_specs, out_specs=out_specs, check_vma=False)
```

```python
import functools
import math

import jax
import jax.numpy as jnp
import numpy as np
from jax import lax
from jax.experimental import pallas as pl
from jax.experimental.pallas import tpu as pltpu
from jax.sharding import PartitionSpec as P

LEADS = 2
POOL = 8
LINES = 4
DEEP = 3
MESH = pl.DeviceIdType.MESH
F32 = jnp.float32
BF16 = jnp.bfloat16
ROW_WAYS = (-1, 1)
EDGE_WAYS = tuple((dr, dc) for dr in (-1, 0, 1) for dc in (-1, 1))


def dot(left, right):
    return jnp.dot(left, right, preferred_element_type=F32)


def dot_t(left, right):
    return lax.dot_general(left, right, (((1,), (1,)), ((), ())), preferred_element_type=F32)


def lane_half(shape):
    return lax.broadcasted_iota(jnp.int32, shape, len(shape) - 1) < shape[-1] // 2


def half_norm(vectors, low):
    squares = vectors * vectors
    count = vectors.shape[-1] // 2
    first = jnp.sum(jnp.where(low, squares, 0.0), axis=-1, keepdims=True) / count
    second = jnp.sum(jnp.where(low, 0.0, squares), axis=-1, keepdims=True) / count
    return vectors * jnp.where(low, lax.rsqrt(first + 1e-06), lax.rsqrt(second + 1e-06))


def twice(weight):
    wide = jnp.concatenate([weight, weight], axis=1)
    low = lane_half(wide.shape)
    return jnp.concatenate([jnp.where(low, wide, 0.0), jnp.where(low, 0.0, wide)], axis=0)


def attend_column(own, every, mix_ref, gain, out_weight):
    lanes = own.shape[-1]
    low = lane_half(own.shape)
    queries = half_norm(dot_t(own, mix_ref[0]), low) * gain
    turned = pltpu.roll(queries, lanes // 2, 1)
    stacked = jnp.concatenate(
        [
            jnp.where(low, queries, 0.0),
            jnp.where(low, turned, 0.0),
            jnp.where(low, 0.0, turned),
            jnp.where(low, 0.0, queries),
        ],
        axis=0,
    ).astype(BF16)
    keys = half_norm(dot_t(every, mix_ref[1]), lane_half(every.shape)).astype(BF16)
    values = dot_t(every, mix_ref[2]).astype(BF16)
    scores = dot_t(stacked, keys) * (1.0 / math.sqrt(lanes // 2))
    count = own.shape[0]
    query_column = lax.broadcasted_iota(jnp.int32, scores.shape, 0) // 8 % 2
    key_column = lax.broadcasted_iota(jnp.int32, scores.shape, 1) // 8 % 2
    scores = jnp.where(query_column == key_column, scores, -1e30)
    highest = jnp.max(scores, axis=1, keepdims=True)
    highest = jnp.maximum(highest[: 2 * count], highest[2 * count :])
    weights = jnp.exp(scores - jnp.concatenate([highest, highest], axis=0))
    mass = jnp.sum(weights, axis=1, keepdims=True)
    mass = mass[: 2 * count] + mass[2 * count :]
    weighted = dot(weights.astype(BF16), values)
    swapped = pltpu.roll(weighted, lanes // 2, 1)
    mixed = jnp.where(
        low,
        (weighted[:count] + swapped[2 * count : 3 * count]) / mass[:count],
        (swapped[count : 2 * count] + weighted[3 * count :]) / mass[count:],
    )
    return own.astype(F32) + dot_t(mixed.astype(BF16), out_weight)


def depthwise(x_ref, taps_ref, spatial_ref, blocks, bands):
    cols = x_ref.shape[2]

    def block(index, carry):
        lo = pl.multiple_of(index * 16, 16)
        taps = [taps_ref[k, pl.ds(lo, 16), :][None] for k in range(9)]
        for start, count in bands:
            rows = x_ref[start : start + count + 2, pl.ds(lo, 16), :]
            left, middle, right = (
                taps[b] * rows[:count]
                + taps[3 + b] * rows[1 : count + 1]
                + taps[6 + b] * rows[2 : count + 2]
                for b in range(3)
            )
            lane = lax.broadcasted_iota(jnp.int32, (count * 16, cols), 1)
            left = pltpu.roll(left.reshape(count * 16, cols), 1, 1)
            right = pltpu.roll(right.reshape(count * 16, cols), cols - 1, 1)
            total = (
                jnp.where(lane == 0, 0.0, left)
                + middle.reshape(count * 16, cols)
                + jnp.where(lane == cols - 1, 0.0, right)
            ).astype(BF16)
            for j in range(count):
                row = start + j
                spatial_ref[row // 2, pl.ds(lo, 16), (row % 2) * cols : (row % 2 + 1) * cols] = (
                    total[j * 16 : (j + 1) * 16]
                )
        return carry

    lax.fori_loop(blocks[0], blocks[1], block, None)


def halo_column(frame_tiles, hidden_tiles, way, masks, taps_t, pad_ref, extra):
    seen, above, below = masks
    first = 8 if way == 1 else 0
    slot = {dr: EDGE_WAYS.index((dr, way)) for dr in (-1, 0, 1)}

    def part(dr):
        frame = frame_tiles(slot[dr]).astype(F32)[first : first + 8]
        hidden = hidden_tiles(dr, way, first)
        low = lane_half(frame.shape)
        half = frame.shape[1] // 2
        upper = jnp.where(low, frame, pltpu.roll(hidden, half, 1))
        lower = jnp.where(low, pltpu.roll(frame, half, 1), hidden)
        return jnp.where(seen, upper, 0.0), jnp.where(seen, lower, 0.0)

    upper, lower = part(0)
    pad_ref[0:8] = jnp.where(above, part(1)[1], 0.0)
    pad_ref[8:16] = upper
    pad_ref[16:24] = lower
    pad_ref[24:32] = jnp.where(below, part(-1)[0], 0.0)
    b = 0 if way == 1 else 2
    rows = [pad_ref[7 + a - extra : 23 + a + extra] for a in range(3)]
    return sum(taps_t[3 * a + b] * rows[a] for a in range(3))


def kernel(
    n_rows,
    n_cols,
    groups,
    members,
    frames_ref,
    hidden_ref,
    cell_ref,
    spread_ref,
    pick_ref,
    depth_ref,
    point_ref,
    bias_ref,
    mixing_ref,
    gain_ref,
    output_ref,
    hidden_out,
    cell_out,
    attended_out,
    point_in,
    depth_in,
    bias_in,
    mixing_in,
    gain_in,
    output_in,
    pick_in,
    frames_in,
    hidden_in,
    cell_now,
    plain,
    x0,
    x1,
    taps,
    spatial0,
    spatial1,
    weight,
    stacked,
    row_out,
    row_in,
    cell_sent,
    cell_rim,
    edge_out0,
    edge_in0,
    stacked_rim,
    edge_out1,
    edge_in1,
    pad,
    mix,
    out_mix,
    given,
    column,
    gathered,
    result,
    returned,
    local_sem,
    send_row,
    recv_row,
    send_edge,
    recv_edge,
    send_side,
    recv_side,
    send_a,
    recv_a,
    send_b,
    recv_b,
    send_c,
    recv_c,
    send_d,
    recv_d,
):
    row, col = lax.axis_index("rows"), lax.axis_index("cols")
    core, group, line = row % 2, row // 2 % groups, row // (2 * groups)
    member = line * 2 + core
    channels = hidden_in.shape[0] // 16
    both = 2 * channels
    cols = hidden_in.shape[1]

    def near(dr, dc):
        return ((row + dr + n_rows) % n_rows, (col + dc + n_cols) % n_cols)

    def mate(step):
        target = (member + step) % members
        return ((target // 2 * groups + group) * 2 + target % 2, col)

    span = groups // DEEP
    level, place_y = group // span, group % span

    def upper(step):
        return ((line * groups + (level + step) % DEEP * span + place_y) * 2 + core, col)

    def twin(step):
        return ((line * groups + level * span + (place_y + step) % span) * 2 + core, col)

    loads = [
        pltpu.make_async_copy(frames_ref.at[0], frames_in.at[0], local_sem.at[0]),
        pltpu.make_async_copy(hidden_ref, hidden_in, local_sem.at[1]),
        pltpu.make_async_copy(frames_ref.at[1], frames_in.at[1], local_sem.at[2]),
        pltpu.make_async_copy(cell_ref, cell_now, local_sem.at[3]),
        pltpu.make_async_copy(spread_ref, spatial0.at[:, both:], local_sem.at[4]),
        pltpu.make_async_copy(spread_ref.at[:8], spatial1.at[:, both:], local_sem.at[5]),
    ]
    small = [
        pltpu.make_async_copy(source, target, local_sem.at[8 + k])
        for k, (source, target) in enumerate(
            (
                (pick_ref, pick_in),
                (depth_ref, depth_in),
                (point_ref, point_in),
                (bias_ref, bias_in),
                (mixing_ref, mixing_in),
                (gain_ref, gain_in),
                (output_ref, output_in),
            )
        )
    ]
    for load in loads[:1] + small[:1] + loads[1:] + small[1:]:
        load.start()

    barrier = pltpu.get_barrier_semaphore()
    peers = [near(dr, dc) for dr, dc in EDGE_WAYS] + [near(dr, 0) for dr in ROW_WAYS]
    peers += [upper(step) for step in range(1, DEEP)] + [twin(step) for step in range(1, span)]
    peers += [mate(step) for step in range(1, members)]
    for peer in peers:
        pl.semaphore_signal(barrier, inc=1, device_id=peer, device_id_type=MESH)

    small[0].wait()
    pick_edges = pick_in[16:, :]
    for k, (source, load) in enumerate(
        ((frames_in.at[0], loads[0]), (hidden_in, loads[1]), (frames_in.at[1], loads[2]))
    ):
        load.wait()
        plain[...] = source[...].astype(F32)
        target, base, first = ((x0, 0, 2), (x0, channels, 2), (x1, 0, 1))[k]
        for r in range(16):
            plane = plain[pl.ds(r, channels, stride=16), :]
            target[r + first, base : base + channels, :] = plane
            low = plane.astype(BF16)
            stacked[
                (r // 8) * channels : (r // 8 + 1) * channels, (r % 8) * cols : (r % 8 + 1) * cols
            ] = low
            if r in (0, 15):
                row_out[r // 15, k * channels : (k + 1) * channels, :] = low
            if r in (1, 14) and k < 2:
                row_out[r // 14, (3 + k) * channels : (4 + k) * channels, :] = low
        edge_out0[k] = dot_t(pick_edges, stacked[...]).astype(BF16)
    loads[3].wait()
    for k, r in enumerate((0, 15)):
        cell_sent[k] = cell_now[pl.ds(r, channels, stride=16), :]

    pl.semaphore_wait(barrier, len(peers))
    sends = []

    def settle(keep):
        done = len(sends) - keep
        for copy in sends[:done]:
            copy.wait_send()
        del sends[:done]

    def send(source, target, send_sem, recv_sem, device):
        copy = pltpu.make_async_remote_copy(
            src_ref=source,
            dst_ref=target,
            send_sem=send_sem,
            recv_sem=recv_sem,
            device_id=device,
            device_id_type=MESH,
        )
        copy.start()
        sends.append(copy)
        return copy

    row_copies, cell_copies, edge_copies = [], [], []
    for k, (dr, dc) in enumerate(EDGE_WAYS):
        edge_copies.append(
            send(edge_out0, edge_in0.at[k], send_edge.at[k], recv_edge.at[k], near(dr, dc))
        )
    for k, dr in enumerate(ROW_WAYS):
        row_copies.append(
            send(row_out.at[k], row_in.at[k], send_row.at[0, k], recv_row.at[0, k], near(dr, 0))
        )
    for k, dr in enumerate(ROW_WAYS):
        cell_copies.append(
            send(cell_sent.at[k], cell_rim.at[k], send_row.at[1, k], recv_row.at[1, k], near(dr, 0))
        )

    for load in small[1:]:
        load.wait()
    taps_t = [depth_in[k // 3, k % 3 : k % 3 + 1, :] for k in range(9)]
    depth = jnp.transpose(jnp.concatenate(taps_t + [jnp.zeros((both - 9, both), F32)], axis=0))
    for k in range(9):
        taps[k] = jnp.broadcast_to(depth[:, k : k + 1], (both, cols))
    lane = lax.broadcasted_iota(jnp.int32, (4 * channels, cols), 1)
    sublane = lax.broadcasted_iota(jnp.int32, (4 * channels, cols), 0)
    halve = jnp.where(sublane < 3 * channels, 0.5, 1.0)
    bias = jnp.transpose(jnp.broadcast_to(bias_in[...], (cols, 4 * channels))) * halve
    weight[:, :both] = (point_in[...].astype(F32) * halve).astype(BF16)
    for part in range(3):
        rounded = bias.astype(BF16).astype(F32)
        bias_lanes = rounded if part == 0 else jnp.where(lane == 72 + part, rounded, bias_lanes)
        bias = bias - rounded
    bias_lanes = jnp.where(lane < 75, bias_lanes, 0.0)
    mixing = jnp.transpose(mixing_in[...].astype(F32))
    for k in range(3):
        mix[k] = twice(mixing[k * channels : (k + 1) * channels]).astype(BF16)
    out_mix[...] = twice(output_in[...].astype(F32)).astype(BF16)
    side_lane = lax.broadcasted_iota(jnp.int32, (16, cols), 1)
    side_row = lax.broadcasted_iota(jnp.int32, (16, cols), 0)
    pick_sides = jnp.where(
        side_lane == side_row * (cols - 1), jnp.where(side_row < 2, 1.0, 0.0), 0.0
    ).astype(BF16)
    gain = jnp.concatenate([gain_in[...], gain_in[...]], axis=1)

    above, below = row > 0, row < n_rows - 1
    interior0, rim0 = ((2, 4), (6, 4), (10, 4), (14, 2)), ((0, 2), (16, 2))
    interior, rim = ((1, 4), (5, 4), (9, 4), (13, 2)), ((0, 1), (15, 1))
    whole = channels // 16
    depthwise(x0, taps, spatial0, (0, 2 * whole), interior0)
    depthwise(x1, taps, spatial1, (0, whole), interior)

    def fill_row(x_ref, place, base, valid, plane):
        x_ref[place, base : base + channels, :] = jnp.where(valid, plane.astype(F32), 0.0)

    def extend(frame_tiles, hidden_tiles, extra):
        left = halo_column(
            frame_tiles, hidden_tiles, 1, (col > 0, above, below), taps_t, pad, extra
        )
        right = halo_column(
            frame_tiles, hidden_tiles, -1, (col < n_cols - 1, above, below), taps_t, pad, extra
        )
        short = jnp.zeros((2 - 2 * extra, both), F32)
        added = [left, short, right, short] if extra == 0 else [left, right]
        rest = jnp.zeros((cols - 72, both), F32)
        added = jnp.concatenate(added + added + [rest], axis=0).astype(BF16)
        lifted = dot_t(weight[:, :both], added)
        rounded = lifted.astype(BF16).astype(F32)
        weight[:, both:] = jnp.where(
            lane < 36, rounded, jnp.where(lane < 72, lifted - rounded, bias_lanes)
        ).astype(BF16)

    def update(step, spatial):
        for pair in range(9 - step):
            gates = dot(weight[...], spatial[pair])
            for j in range(2):
                r = 2 * pair + j - 1 + step
                in_gate, forget, out_gate, candidate = (
                    jnp.tanh(gates[k * channels : (k + 1) * channels, j * cols : (j + 1) * cols])
                    for k in range(4)
                )
                outside = r < 0 or r > 15
                place = pl.ds(r, channels, stride=16)
                before = cell_rim[1 if r < 0 else 0] if outside else cell_now[place, :]
                memory = (0.5 * forget + 0.5) * before + (0.5 * in_gate + 0.5) * candidate
                hidden = (0.5 * out_gate + 0.5) * jnp.tanh(memory)
                low = hidden.astype(BF16)
                if outside:
                    fill_row(x1, r + 1, channels, above if r < 0 else below, low)
                    half = 1 if r < 0 else 0
                    stacked_rim[half * channels : (half + 1) * channels, :] = low
                    continue
                cell_now[place, :] = memory
                stacked[
                    (r // 8) * channels : (r // 8 + 1) * channels,
                    (r % 8) * cols : (r % 8 + 1) * cols,
                ] = low
                if step == 0:
                    x1[r + 1, channels:both, :] = low.astype(F32)
                else:
                    plain[place, :] = hidden

    def share(lead, pooled):
        pooled = pooled.astype(BF16).astype(F32)
        for k in range(members):
            given[lead, k] = pooled[2 * k : 2 * k + 2]
        column[lead, member] = given[lead, member]
        copies = []
        for step in range(1, members):
            copies.append(
                send(
                    given.at[lead, (member + step) % members],
                    column.at[lead, member],
                    send_a.at[lead, step],
                    recv_a.at[lead, step],
                    mate(step),
                )
            )
        return copies

    def gather(lead, copies):
        for copy in copies:
            copy.wait_recv()
        gathered[lead, place_y, level] = jnp.concatenate(
            [column[lead, :, k, :] for k in range(2)], axis=0
        ).astype(BF16)
        return [
            send(
                gathered.at[lead, place_y, level],
                gathered.at[lead, place_y, level],
                send_b.at[lead, step],
                recv_b.at[lead, step],
                upper(step),
            )
            for step in range(1, DEEP)
        ]

    def spread(lead, copies):
        for copy in copies:
            copy.wait_recv()
        return [
            send(
                gathered.at[lead, place_y],
                gathered.at[lead, place_y],
                send_d.at[lead, step],
                recv_d.at[lead, step],
                twin(step),
            )
            for step in range(1, span)
        ]

    def attend(lead, copies):
        for copy in copies:
            copy.wait_recv()
        attended = attend_column(
            gathered[lead, place_y, level],
            gathered[lead].reshape(groups * 2 * members, both),
            mix,
            gain,
            out_mix[...],
        )
        for k in range(2):
            result[lead, :, k, :] = attended[k * members : (k + 1) * members]
        returned[lead, member] = result[lead, member]
        copies = []
        for step in range(1, members):
            copies.append(
                send(
                    result.at[lead, (member + step) % members],
                    returned.at[lead, member],
                    send_c.at[lead, step],
                    recv_c.at[lead, step],
                    mate(step),
                )
            )
        return copies

    def plane(k, index):
        return row_in[k, index * channels : (index + 1) * channels, :]

    def first_hidden(dr, way, first):
        return edge_in0[EDGE_WAYS.index((dr, way)), 1].astype(F32)[first : first + 8]

    def second_hidden(dr, way, first):
        tile = edge_in1[0 if way == -1 else 1].astype(F32)
        if dr == 0:
            return tile[first : first + 8]
        return jnp.broadcast_to(tile[16 + first // 8 : 17 + first // 8], (8, both))

    for copy in edge_copies + row_copies:
        copy.wait_recv()
    for k in range(2):
        fill_row(x0, 0, k * channels, above, plane(1, 3 + k))
        fill_row(x0, 1, k * channels, above, plane(1, k))
        fill_row(x0, 18, k * channels, below, plane(0, k))
        fill_row(x0, 19, k * channels, below, plane(0, 3 + k))
    depthwise(x0, taps, spatial0, (0, 2 * whole), rim0)
    extend(lambda k: edge_in0[k, 0], first_hidden, 1)
    for load in loads[4:]:
        load.wait()
    for copy in cell_copies:
        copy.wait_recv()
    update(0, spatial0)
    picked = dot_t(pick_in[...], stacked[...])
    edge_out1[0:16] = picked[16:].astype(BF16)
    edge_out1[16:32] = dot_t(pick_sides, stacked_rim[...]).astype(BF16)
    side_copies = []
    for k, dc in enumerate((-1, 1)):
        side_copies.append(
            send(edge_out1, edge_in1.at[k], send_side.at[k], recv_side.at[k], near(0, dc))
        )
    shared0 = share(0, picked[:16])
    fill_row(x1, 0, 0, above, plane(1, 2))
    fill_row(x1, 17, 0, below, plane(0, 2))
    depthwise(x1, taps, spatial1, (0, whole), rim)
    depthwise(x1, taps, spatial1, (whole, 2 * whole), interior + rim)
    for copy in side_copies:
        copy.wait_recv()
    extend(lambda k: edge_in0[k, 2], second_hidden, 0)
    gathered0 = gather(0, shared0)
    update(1, spatial1)
    picked = dot_t(pick_in[:16, :], stacked[...])
    shared1 = share(1, picked)
    spread0 = spread(0, gathered0)
    settle(len(shared1) + len(spread0))
    store_cell = pltpu.make_async_copy(cell_now, cell_out, local_sem.at[6])
    store_cell.start()
    hidden_in[...] = plain[...].astype(BF16)
    store_hidden = pltpu.make_async_copy(hidden_in, hidden_out, local_sem.at[7])
    store_hidden.start()
    gathered1 = gather(1, shared1)
    returned0 = attend(0, spread0)
    spread1 = spread(1, gathered1)
    settle(len(spread1))
    returned1 = attend(1, spread1)
    for lead, copies in enumerate((returned0, returned1)):
        for copy in copies:
            copy.wait_recv()
        attended = jnp.concatenate([returned[lead, k] for k in range(members)], axis=0)
        for k in range(2):
            attended_out[lead, k] = attended[:, k * channels : (k + 1) * channels]
    store_cell.wait()
    store_hidden.wait()
    settle(0)


def finish_kernel(*refs):
    count = (len(refs) - 1) // 3
    sources, targets, held, sem = refs[:count], refs[count : 2 * count], refs[2 * count : -1], refs[-1]
    loads = [pltpu.make_async_copy(sources[k], held[k], sem.at[0, k]) for k in range(count)]
    stores = [pltpu.make_async_copy(held[k], targets[k], sem.at[1, k]) for k in range(count)]
    for load in loads:
        load.start()
    for load, store in zip(loads, stores):
        load.wait()
        store.start()
    for store in stores:
        store.wait()


def finish(*arrays):
    hbm = pl.BlockSpec(memory_space=pltpu.HBM)
    return pl.pallas_call(
        finish_kernel,
        out_shape=tuple(jax.ShapeDtypeStruct(a.shape, a.dtype) for a in arrays),
        in_specs=[hbm] * len(arrays),
        out_specs=(hbm,) * len(arrays),
        scratch_shapes=[pltpu.VMEM(a.shape, a.dtype) for a in arrays]
        + [pltpu.SemaphoreType.DMA((2, len(arrays)))],
        compiler_params=pltpu.CompilerParams(vmem_limit_bytes=60 * 2**20),
    )(*arrays)


def picker(cols):
    pick = np.zeros((32, POOL, cols), np.float32)
    for k in range(cols // POOL):
        pick[k, :, k * POOL : (k + 1) * POOL] = 1.0 / (POOL * POOL)
    for r in range(POOL):
        pick[16 + r, r, 0] = 1.0
        pick[24 + r, r, cols - 1] = 1.0
    return pick.reshape(32, POOL * cols)


def spreader(cols):
    spread = np.zeros((9, 128, 2, cols), np.float32)
    for pair in range(9):
        for j in range(2):
            r = 2 * pair + j
            for twin in (0, 36):
                spread[pair, twin + r, j, 0] = 1.0
                spread[pair, twin + 18 + r, j, cols - 1] = 1.0
    spread[:, 72:75] = 1.0
    return spread.reshape(9, 128, 2 * cols)


def body(
    frames,
    hidden_state,
    cell_state,
    depth_kernel,
    point_weight,
    gate_bias,
    mixing_weight,
    query_gain,
    output_weight,
):
    channels, row_count, cols = hidden_state.shape
    both = 2 * channels
    flat = channels * row_count
    n_rows, n_cols = lax.axis_size("rows"), lax.axis_size("cols")
    members = 2 * LINES
    groups = n_rows // members
    hbm = pl.BlockSpec(memory_space=pltpu.HBM)
    any_space = pl.BlockSpec(memory_space=pl.ANY)
    vmem = pl.BlockSpec(memory_space=pltpu.VMEM)
    dma = pltpu.SemaphoreType.DMA
    hidden, cell, attended = pl.pallas_call(
        functools.partial(kernel, n_rows, n_cols, groups, members),
        out_shape=(
            jax.ShapeDtypeStruct((flat, cols), BF16),
            jax.ShapeDtypeStruct((flat, cols), F32),
            jax.ShapeDtypeStruct((LEADS, 2, cols // POOL, channels), F32),
        ),
        in_specs=[hbm] * 11,
        out_specs=(any_space, any_space, vmem),
        scratch_shapes=[
            pltpu.VMEM((4 * channels, both), BF16),
            pltpu.VMEM((3, 3, both), F32),
            pltpu.VMEM((1, 4 * channels), F32),
            pltpu.VMEM((channels, 3 * channels), BF16),
            pltpu.VMEM((1, channels), F32),
            pltpu.VMEM((channels, channels), BF16),
            pltpu.VMEM((32, POOL * cols), BF16),
            pltpu.VMEM((LEADS, flat, cols), BF16),
            pltpu.VMEM((flat, cols), BF16),
            pltpu.VMEM((flat, cols), F32),
            pltpu.VMEM((flat, cols), F32),
            pltpu.VMEM((row_count + 4, both, cols), F32),
            pltpu.VMEM((row_count + 2, both, cols), F32),
            pltpu.VMEM((9, both, cols), F32),
            pltpu.VMEM((9, 2 * both, 2 * cols), BF16),
            pltpu.VMEM((8, 2 * both, 2 * cols), BF16),
            pltpu.VMEM((4 * channels, 2 * both), BF16),
            pltpu.VMEM((both, POOL * cols), BF16),
            pltpu.VMEM((2, 5 * channels, cols), BF16),
            pltpu.VMEM((2, 5 * channels, cols), BF16),
            pltpu.VMEM((2, channels, cols), F32),
            pltpu.VMEM((2, channels, cols), F32),
            pltpu.VMEM((3, 16, both), BF16),
            pltpu.VMEM((6, 3, 16, both), BF16),
            pltpu.VMEM((both, cols), BF16),
            pltpu.VMEM((32, both), BF16),
            pltpu.VMEM((2, 32, both), BF16),
            pltpu.VMEM((32, both), F32),
            pltpu.VMEM((3, both, both), BF16),
            pltpu.VMEM((both, both), BF16),
            pltpu.VMEM((LEADS, members, 2, both), F32),
            pltpu.VMEM((LEADS, members, 2, both), F32),
            pltpu.VMEM((LEADS, groups // DEEP, DEEP, 2 * members, both), BF16),
            pltpu.VMEM((LEADS, members, 2, both), F32),
            pltpu.VMEM((LEADS, members, 2, both), F32),
            dma((15,)),
            dma((2, 2)),
            dma((2, 2)),
            dma((6,)),
            dma((6,)),
            dma((2,)),
            dma((2,)),
            dma((LEADS, members)),
            dma((LEADS, members)),
            dma((LEADS, DEEP)),
            dma((LEADS, DEEP)),
            dma((LEADS, members)),
            dma((LEADS, members)),
            dma((LEADS, groups // DEEP)),
            dma((LEADS, groups // DEEP)),
        ],
        compiler_params=pltpu.CompilerParams(
            collective_id=0, has_side_effects=True, vmem_limit_bytes=60 * 2**20
        ),
    )(
        frames.reshape(LEADS, flat, cols),
        hidden_state.reshape(flat, cols),
        cell_state.reshape(flat, cols),
        jnp.asarray(spreader(cols), BF16),
        jnp.asarray(picker(cols), BF16),
        jnp.transpose(depth_kernel, (1, 2, 0)),
        point_weight,
        gate_bias[None],
        mixing_weight.T,
        query_gain[None],
        output_weight,
    )
    attended, cell, hidden = finish(attended, cell, hidden)
    attended = jnp.transpose(attended, (0, 3, 1, 2))
    shape = (channels, row_count, cols)
    return (hidden.reshape(shape), cell.reshape(shape), attended)


def solution(mesh):
    in_specs = (
        P(None, None, "rows", "cols"),
        P(None, "rows", "cols"),
        P(None, "rows", "cols"),
        P(),
        P(),
        P(),
        P(),
        P(),
        P(),
    )
    out_specs = (P(None, "rows", "cols"), P(None, "rows", "cols"), P(None, None, "rows", "cols"))
    return jax.shard_map(body, mesh=mesh, in_specs=in_specs, out_specs=out_specs, check_vma=False)
```

```python
import functools
import math

import jax
import jax.numpy as jnp
import numpy as np
from jax import lax
from jax.experimental import pallas as pl
from jax.experimental.pallas import tpu as pltpu
from jax.sharding import PartitionSpec as P

LEADS = 2
POOL = 8
LINES = 4
DEEP = 3
MESH = pl.DeviceIdType.MESH
F32 = jnp.float32
BF16 = jnp.bfloat16
ROW_WAYS = (-1, 1)
EDGE_WAYS = tuple((dr, dc) for dr in (-1, 0, 1) for dc in (-1, 1))


def dot(left, right):
    return jnp.dot(left, right, preferred_element_type=F32)


def dot_t(left, right):
    return lax.dot_general(left, right, (((1,), (1,)), ((), ())), preferred_element_type=F32)


def lane_half(shape):
    return lax.broadcasted_iota(jnp.int32, shape, len(shape) - 1) < shape[-1] // 2


def half_norm(vectors, low):
    squares = vectors * vectors
    count = vectors.shape[-1] // 2
    first = jnp.sum(jnp.where(low, squares, 0.0), axis=-1, keepdims=True) / count
    second = jnp.sum(jnp.where(low, 0.0, squares), axis=-1, keepdims=True) / count
    return vectors * jnp.where(low, lax.rsqrt(first + 1e-06), lax.rsqrt(second + 1e-06))


def twice(weight):
    wide = jnp.concatenate([weight, weight], axis=1)
    low = lane_half(wide.shape)
    return jnp.concatenate([jnp.where(low, wide, 0.0), jnp.where(low, 0.0, wide)], axis=0)


def attend_column(own, every, mix_ref, gain, out_weight):
    lanes = own.shape[-1]
    low = lane_half(own.shape)
    queries = half_norm(dot_t(own, mix_ref[0]), low) * gain
    turned = pltpu.roll(queries, lanes // 2, 1)
    stacked = jnp.concatenate(
        [
            jnp.where(low, queries, 0.0),
            jnp.where(low, turned, 0.0),
            jnp.where(low, 0.0, turned),
            jnp.where(low, 0.0, queries),
        ],
        axis=0,
    ).astype(BF16)
    keys = half_norm(dot_t(every, mix_ref[1]), lane_half(every.shape)).astype(BF16)
    values = dot_t(every, mix_ref[2]).astype(BF16)
    scores = dot_t(stacked, keys) * (1.0 / math.sqrt(lanes // 2))
    count = own.shape[0]
    query_column = lax.broadcasted_iota(jnp.int32, scores.shape, 0) // 8 % 2
    key_column = lax.broadcasted_iota(jnp.int32, scores.shape, 1) // 8 % 2
    scores = jnp.where(query_column == key_column, scores, -1e30)
    highest = jnp.max(scores, axis=1, keepdims=True)
    highest = jnp.maximum(highest[: 2 * count], highest[2 * count :])
    weights = jnp.exp(scores - jnp.concatenate([highest, highest], axis=0))
    mass = jnp.sum(weights, axis=1, keepdims=True)
    mass = mass[: 2 * count] + mass[2 * count :]
    weighted = dot(weights.astype(BF16), values)
    swapped = pltpu.roll(weighted, lanes // 2, 1)
    mixed = jnp.where(
        low,
        (weighted[:count] + swapped[2 * count : 3 * count]) / mass[:count],
        (swapped[count : 2 * count] + weighted[3 * count :]) / mass[count:],
    )
    return own.astype(F32) + dot_t(mixed.astype(BF16), out_weight)


def depthwise(x_ref, taps_ref, spatial_ref, blocks, bands):
    cols = x_ref.shape[2]

    def block(index, carry):
        lo = pl.multiple_of(index * 16, 16)
        taps = [taps_ref[k, pl.ds(lo, 16), :][None] for k in range(9)]
        for start, count in bands:
            rows = x_ref[start : start + count + 2, pl.ds(lo, 16), :]
            left, middle, right = (
                taps[b] * rows[:count]
                + taps[3 + b] * rows[1 : count + 1]
                + taps[6 + b] * rows[2 : count + 2]
                for b in range(3)
            )
            lane = lax.broadcasted_iota(jnp.int32, (count * 16, cols), 1)
            left = pltpu.roll(left.reshape(count * 16, cols), 1, 1)
            right = pltpu.roll(right.reshape(count * 16, cols), cols - 1, 1)
            total = (
                jnp.where(lane == 0, 0.0, left)
                + middle.reshape(count * 16, cols)
                + jnp.where(lane == cols - 1, 0.0, right)
            ).astype(BF16)
            for j in range(count):
                row = start + j
                spatial_ref[row // 2, pl.ds(lo, 16), (row % 2) * cols : (row % 2 + 1) * cols] = (
                    total[j * 16 : (j + 1) * 16]
                )
        return carry

    lax.fori_loop(blocks[0], blocks[1], block, None)


def halo_column(frame_tiles, hidden_tiles, way, masks, taps_t, pad_ref, extra):
    seen, above, below = masks
    first = 8 if way == 1 else 0
    slot = {dr: EDGE_WAYS.index((dr, way)) for dr in (-1, 0, 1)}

    def part(dr):
        frame = frame_tiles(slot[dr]).astype(F32)[first : first + 8]
        hidden = hidden_tiles(dr, way, first)
        low = lane_half(frame.shape)
        half = frame.shape[1] // 2
        upper = jnp.where(low, frame, pltpu.roll(hidden, half, 1))
        lower = jnp.where(low, pltpu.roll(frame, half, 1), hidden)
        return jnp.where(seen, upper, 0.0), jnp.where(seen, lower, 0.0)

    upper, lower = part(0)
    pad_ref[0:8] = jnp.where(above, part(1)[1], 0.0)
    pad_ref[8:16] = upper
    pad_ref[16:24] = lower
    pad_ref[24:32] = jnp.where(below, part(-1)[0], 0.0)
    b = 0 if way == 1 else 2
    rows = [pad_ref[7 + a - extra : 23 + a + extra] for a in range(3)]
    return sum(taps_t[3 * a + b] * rows[a] for a in range(3))


def kernel(
    n_rows,
    n_cols,
    groups,
    members,
    frames_ref,
    hidden_ref,
    cell_ref,
    spread_ref,
    pick_ref,
    depth_ref,
    point_ref,
    bias_ref,
    mixing_ref,
    gain_ref,
    output_ref,
    hidden_out,
    cell_out,
    attended_out,
    point_in,
    depth_in,
    bias_in,
    mixing_in,
    gain_in,
    output_in,
    pick_in,
    frames_in,
    hidden_in,
    cell_now,
    plain,
    x0,
    x1,
    taps,
    spatial0,
    spatial1,
    weight,
    stacked,
    row_out,
    row_in,
    cell_sent,
    cell_rim,
    edge_out0,
    edge_in0,
    stacked_rim,
    edge_out1,
    edge_in1,
    pad,
    mix,
    out_mix,
    given,
    column,
    gathered,
    result,
    returned,
    local_sem,
    halo_send,
    halo_recv,
    send_a,
    recv_a,
    send_b,
    recv_b,
    send_c,
    recv_c,
    send_d,
    recv_d,
):
    row, col = lax.axis_index("rows"), lax.axis_index("cols")
    core, group, line = row % 2, row // 2 % groups, row // (2 * groups)
    member = line * 2 + core
    channels = hidden_in.shape[0] // 16
    both = 2 * channels
    cols = hidden_in.shape[1]

    def near(dr, dc):
        return ((row + dr + n_rows) % n_rows, (col + dc + n_cols) % n_cols)

    def mate(step):
        target = (member + step) % members
        return ((target // 2 * groups + group) * 2 + target % 2, col)

    span = groups // DEEP
    level, place_y = group // span, group % span

    def upper(step):
        return ((line * groups + (level + step) % DEEP * span + place_y) * 2 + core, col)

    def twin(step):
        return ((line * groups + level * span + (place_y + step) % span) * 2 + core, col)

    loads = [
        pltpu.make_async_copy(frames_ref.at[0], frames_in.at[0], local_sem.at[0]),
        pltpu.make_async_copy(hidden_ref, hidden_in, local_sem.at[1]),
        pltpu.make_async_copy(frames_ref.at[1], frames_in.at[1], local_sem.at[2]),
        pltpu.make_async_copy(cell_ref, cell_now, local_sem.at[3]),
        pltpu.make_async_copy(spread_ref, spatial0.at[:, both:], local_sem.at[4]),
        pltpu.make_async_copy(spread_ref.at[:8], spatial1.at[:, both:], local_sem.at[5]),
    ]
    small = [
        pltpu.make_async_copy(source, target, local_sem.at[8 + k])
        for k, (source, target) in enumerate(
            (
                (pick_ref, pick_in),
                (depth_ref, depth_in),
                (point_ref, point_in),
                (bias_ref, bias_in),
                (mixing_ref, mixing_in),
                (gain_ref, gain_in),
                (output_ref, output_in),
            )
        )
    ]
    for load in loads[:1] + small[:1] + loads[1:] + small[1:]:
        load.start()

    barrier = pltpu.get_barrier_semaphore()
    peers = [near(dr, dc) for dr, dc in EDGE_WAYS] + [near(dr, 0) for dr in ROW_WAYS]
    peers += [upper(step) for step in range(1, DEEP)] + [twin(step) for step in range(1, span)]
    peers += [mate(step) for step in range(1, members)]
    for peer in peers:
        pl.semaphore_signal(barrier, inc=1, device_id=peer, device_id_type=MESH)

    small[0].wait()
    pick_edges = pick_in[16:, :]
    for k, (source, load) in enumerate(
        ((frames_in.at[0], loads[0]), (hidden_in, loads[1]), (frames_in.at[1], loads[2]))
    ):
        load.wait()
        plain[...] = source[...].astype(F32)
        target, base, first = ((x0, 0, 2), (x0, channels, 2), (x1, 0, 1))[k]
        for r in range(16):
            plane = plain[pl.ds(r, channels, stride=16), :]
            target[r + first, base : base + channels, :] = plane
            low = plane.astype(BF16)
            stacked[
                (r // 8) * channels : (r // 8 + 1) * channels, (r % 8) * cols : (r % 8 + 1) * cols
            ] = low
            if r in (0, 15):
                row_out[r // 15, k * channels : (k + 1) * channels, :] = low
            if r in (1, 14) and k < 2:
                row_out[r // 14, (3 + k) * channels : (4 + k) * channels, :] = low
        edge_out0[k] = dot_t(pick_edges, stacked[...]).astype(BF16)
    loads[3].wait()
    for k, r in enumerate((0, 15)):
        cell_sent[k] = cell_now[pl.ds(r, channels, stride=16), :]

    pl.semaphore_wait(barrier, len(peers))
    sends = []

    def settle(keep):
        done = len(sends) - keep
        for ref, sem in sends[:done]:
            arrive(ref, sem)
        del sends[:done]

    def arrive(ref, sem):
        pltpu.make_async_copy(ref, ref, sem).wait()

    def send(source, target, send_sem, recv_sem, device):
        copy = pltpu.make_async_remote_copy(
            src_ref=source,
            dst_ref=target,
            send_sem=send_sem,
            recv_sem=recv_sem,
            device_id=device,
            device_id_type=MESH,
        )
        copy.start()

    for k, (dr, dc) in enumerate(EDGE_WAYS):
        send(edge_out0, edge_in0.at[k], halo_send.at[0], halo_recv.at[0], near(dr, dc))
    for k, dr in enumerate(ROW_WAYS):
        send(row_out.at[k], row_in.at[k], halo_send.at[1], halo_recv.at[1], near(dr, 0))
    for k, dr in enumerate(ROW_WAYS):
        send(cell_sent.at[k], cell_rim.at[k], halo_send.at[2], halo_recv.at[2], near(dr, 0))
    sends += [(edge_in0, halo_send.at[0]), (row_out, halo_send.at[1]), (cell_sent, halo_send.at[2])]

    for load in small[1:]:
        load.wait()
    taps_t = [depth_in[k // 3, k % 3 : k % 3 + 1, :] for k in range(9)]
    depth = jnp.transpose(jnp.concatenate(taps_t + [jnp.zeros((both - 9, both), F32)], axis=0))
    for k in range(9):
        taps[k] = jnp.broadcast_to(depth[:, k : k + 1], (both, cols))
    lane = lax.broadcasted_iota(jnp.int32, (4 * channels, cols), 1)
    sublane = lax.broadcasted_iota(jnp.int32, (4 * channels, cols), 0)
    halve = jnp.where(sublane < 3 * channels, 0.5, 1.0)
    bias = jnp.transpose(jnp.broadcast_to(bias_in[...], (cols, 4 * channels))) * halve
    weight[:, :both] = (point_in[...].astype(F32) * halve).astype(BF16)
    for part in range(3):
        rounded = bias.astype(BF16).astype(F32)
        bias_lanes = rounded if part == 0 else jnp.where(lane == 72 + part, rounded, bias_lanes)
        bias = bias - rounded
    bias_lanes = jnp.where(lane < 75, bias_lanes, 0.0)
    mixing = jnp.transpose(mixing_in[...].astype(F32))
    for k in range(3):
        mix[k] = twice(mixing[k * channels : (k + 1) * channels]).astype(BF16)
    out_mix[...] = twice(output_in[...].astype(F32)).astype(BF16)
    side_lane = lax.broadcasted_iota(jnp.int32, (16, cols), 1)
    side_row = lax.broadcasted_iota(jnp.int32, (16, cols), 0)
    pick_sides = jnp.where(
        side_lane == side_row * (cols - 1), jnp.where(side_row < 2, 1.0, 0.0), 0.0
    ).astype(BF16)
    gain = jnp.concatenate([gain_in[...], gain_in[...]], axis=1)

    above, below = row > 0, row < n_rows - 1
    interior0, rim0 = ((2, 4), (6, 4), (10, 4), (14, 2)), ((0, 2), (16, 2))
    interior, rim = ((1, 4), (5, 4), (9, 4), (13, 2)), ((0, 1), (15, 1))
    whole = channels // 16
    depthwise(x0, taps, spatial0, (0, 2 * whole), interior0)
    depthwise(x1, taps, spatial1, (0, whole), interior)

    def fill_row(x_ref, place, base, valid, plane):
        x_ref[place, base : base + channels, :] = jnp.where(valid, plane.astype(F32), 0.0)

    def extend(frame_tiles, hidden_tiles, extra):
        left = halo_column(
            frame_tiles, hidden_tiles, 1, (col > 0, above, below), taps_t, pad, extra
        )
        right = halo_column(
            frame_tiles, hidden_tiles, -1, (col < n_cols - 1, above, below), taps_t, pad, extra
        )
        short = jnp.zeros((2 - 2 * extra, both), F32)
        added = [left, short, right, short] if extra == 0 else [left, right]
        rest = jnp.zeros((cols - 72, both), F32)
        added = jnp.concatenate(added + added + [rest], axis=0).astype(BF16)
        lifted = dot_t(weight[:, :both], added)
        rounded = lifted.astype(BF16).astype(F32)
        weight[:, both:] = jnp.where(
            lane < 36, rounded, jnp.where(lane < 72, lifted - rounded, bias_lanes)
        ).astype(BF16)

    def update(step, spatial):
        for pair in range(9 - step):
            gates = dot(weight[...], spatial[pair])
            for j in range(2):
                r = 2 * pair + j - 1 + step
                in_gate, forget, out_gate, candidate = (
                    jnp.tanh(gates[k * channels : (k + 1) * channels, j * cols : (j + 1) * cols])
                    for k in range(4)
                )
                outside = r < 0 or r > 15
                place = pl.ds(r, channels, stride=16)
                before = cell_rim[1 if r < 0 else 0] if outside else cell_now[place, :]
                memory = (0.5 * forget + 0.5) * before + (0.5 * in_gate + 0.5) * candidate
                hidden = (0.5 * out_gate + 0.5) * jnp.tanh(memory)
                low = hidden.astype(BF16)
                if outside:
                    fill_row(x1, r + 1, channels, above if r < 0 else below, low)
                    half = 1 if r < 0 else 0
                    stacked_rim[half * channels : (half + 1) * channels, :] = low
                    continue
                cell_now[place, :] = memory
                stacked[
                    (r // 8) * channels : (r // 8 + 1) * channels,
                    (r % 8) * cols : (r % 8 + 1) * cols,
                ] = low
                if step == 0:
                    x1[r + 1, channels:both, :] = low.astype(F32)
                else:
                    plain[place, :] = hidden

    def share(lead, pooled):
        pooled = pooled.astype(BF16).astype(F32)
        for k in range(members):
            given[lead, k] = pooled[2 * k : 2 * k + 2]
        column[lead, member] = given[lead, member]
        for step in range(1, members):
            send(
                given.at[lead, (member + step) % members],
                column.at[lead, member],
                send_a.at[lead],
                recv_a.at[lead],
                mate(step),
            )
        sends.append((given.at[lead, 1:], send_a.at[lead]))

    def gather(lead):
        arrive(column.at[lead, 1:], recv_a.at[lead])
        gathered[lead, place_y, level] = jnp.concatenate(
            [column[lead, :, k, :] for k in range(2)], axis=0
        ).astype(BF16)
        for step in range(1, DEEP):
            send(
                gathered.at[lead, place_y, level],
                gathered.at[lead, place_y, level],
                send_b.at[lead],
                recv_b.at[lead],
                upper(step),
            )
        sends.append((gathered.at[lead, 0, 1:], send_b.at[lead]))

    def spread(lead):
        arrive(gathered.at[lead, 0, 1:], recv_b.at[lead])
        for step in range(1, span):
            send(
                gathered.at[lead, place_y],
                gathered.at[lead, place_y],
                send_d.at[lead],
                recv_d.at[lead],
                twin(step),
            )
        sends.append((gathered.at[lead, 1:], send_d.at[lead]))

    def attend(lead):
        arrive(gathered.at[lead, 1:], recv_d.at[lead])
        attended = attend_column(
            gathered[lead, place_y, level],
            gathered[lead].reshape(groups * 2 * members, both),
            mix,
            gain,
            out_mix[...],
        )
        for k in range(2):
            result[lead, :, k, :] = attended[k * members : (k + 1) * members]
        returned[lead, member] = result[lead, member]
        for step in range(1, members):
            send(
                result.at[lead, (member + step) % members],
                returned.at[lead, member],
                send_c.at[lead],
                recv_c.at[lead],
                mate(step),
            )
        sends.append((result.at[lead, 1:], send_c.at[lead]))

    def plane(k, index):
        return row_in[k, index * channels : (index + 1) * channels, :]

    def first_hidden(dr, way, first):
        return edge_in0[EDGE_WAYS.index((dr, way)), 1].astype(F32)[first : first + 8]

    def second_hidden(dr, way, first):
        tile = edge_in1[0 if way == -1 else 1].astype(F32)
        if dr == 0:
            return tile[first : first + 8]
        return jnp.broadcast_to(tile[16 + first // 8 : 17 + first // 8], (8, both))

    arrive(edge_in0, halo_recv.at[0])
    arrive(row_in, halo_recv.at[1])
    for k in range(2):
        fill_row(x0, 0, k * channels, above, plane(1, 3 + k))
        fill_row(x0, 1, k * channels, above, plane(1, k))
        fill_row(x0, 18, k * channels, below, plane(0, k))
        fill_row(x0, 19, k * channels, below, plane(0, 3 + k))
    depthwise(x0, taps, spatial0, (0, 2 * whole), rim0)
    extend(lambda k: edge_in0[k, 0], first_hidden, 1)
    for load in loads[4:]:
        load.wait()
    arrive(cell_rim, halo_recv.at[2])
    update(0, spatial0)
    picked = dot_t(pick_in[...], stacked[...])
    edge_out1[0:16] = picked[16:].astype(BF16)
    edge_out1[16:32] = dot_t(pick_sides, stacked_rim[...]).astype(BF16)
    for k, dc in enumerate((-1, 1)):
        send(edge_out1, edge_in1.at[k], halo_send.at[3], halo_recv.at[3], near(0, dc))
    sends.append((edge_in1, halo_send.at[3]))
    share(0, picked[:16])
    fill_row(x1, 0, 0, above, plane(1, 2))
    fill_row(x1, 17, 0, below, plane(0, 2))
    depthwise(x1, taps, spatial1, (0, whole), rim)
    depthwise(x1, taps, spatial1, (whole, 2 * whole), interior + rim)
    arrive(edge_in1, halo_recv.at[3])
    extend(lambda k: edge_in0[k, 2], second_hidden, 0)
    update(1, spatial1)
    picked = dot_t(pick_in[:16, :], stacked[...])
    share(1, picked)
    gather(0)
    settle(2)
    store_cell = pltpu.make_async_copy(cell_now, cell_out, local_sem.at[6])
    store_cell.start()
    hidden_in[...] = plain[...].astype(BF16)
    store_hidden = pltpu.make_async_copy(hidden_in, hidden_out, local_sem.at[7])
    store_hidden.start()
    gather(1)
    spread(0)
    spread(1)
    attend(0)
    settle(2)
    attend(1)
    for lead in range(LEADS):
        arrive(returned.at[lead, 1:], recv_c.at[lead])
        attended = jnp.concatenate([returned[lead, k] for k in range(members)], axis=0)
        for k in range(2):
            attended_out[lead, k] = attended[:, k * channels : (k + 1) * channels]
    store_cell.wait()
    store_hidden.wait()
    settle(0)


def finish_kernel(*refs):
    count = (len(refs) - 1) // 3
    sources, targets, held, sem = refs[:count], refs[count : 2 * count], refs[2 * count : -1], refs[-1]
    loads = [pltpu.make_async_copy(sources[k], held[k], sem.at[0, k]) for k in range(count)]
    stores = [pltpu.make_async_copy(held[k], targets[k], sem.at[1, k]) for k in range(count)]
    for load in loads:
        load.start()
    for load, store in zip(loads, stores):
        load.wait()
        store.start()
    for store in stores:
        store.wait()


def finish(*arrays):
    hbm = pl.BlockSpec(memory_space=pltpu.HBM)
    return pl.pallas_call(
        finish_kernel,
        out_shape=tuple(jax.ShapeDtypeStruct(a.shape, a.dtype) for a in arrays),
        in_specs=[hbm] * len(arrays),
        out_specs=(hbm,) * len(arrays),
        scratch_shapes=[pltpu.VMEM(a.shape, a.dtype) for a in arrays]
        + [pltpu.SemaphoreType.DMA((2, len(arrays)))],
        compiler_params=pltpu.CompilerParams(vmem_limit_bytes=60 * 2**20),
    )(*arrays)


def picker(cols):
    pick = np.zeros((32, POOL, cols), np.float32)
    for k in range(cols // POOL):
        pick[k, :, k * POOL : (k + 1) * POOL] = 1.0 / (POOL * POOL)
    for r in range(POOL):
        pick[16 + r, r, 0] = 1.0
        pick[24 + r, r, cols - 1] = 1.0
    return pick.reshape(32, POOL * cols)


def spreader(cols):
    spread = np.zeros((9, 128, 2, cols), np.float32)
    for pair in range(9):
        for j in range(2):
            r = 2 * pair + j
            for twin in (0, 36):
                spread[pair, twin + r, j, 0] = 1.0
                spread[pair, twin + 18 + r, j, cols - 1] = 1.0
    spread[:, 72:75] = 1.0
    return spread.reshape(9, 128, 2 * cols)


def body(
    frames,
    hidden_state,
    cell_state,
    depth_kernel,
    point_weight,
    gate_bias,
    mixing_weight,
    query_gain,
    output_weight,
):
    channels, row_count, cols = hidden_state.shape
    both = 2 * channels
    flat = channels * row_count
    n_rows, n_cols = lax.axis_size("rows"), lax.axis_size("cols")
    members = 2 * LINES
    groups = n_rows // members
    hbm = pl.BlockSpec(memory_space=pltpu.HBM)
    any_space = pl.BlockSpec(memory_space=pl.ANY)
    vmem = pl.BlockSpec(memory_space=pltpu.VMEM)
    dma = pltpu.SemaphoreType.DMA
    hidden, cell, attended = pl.pallas_call(
        functools.partial(kernel, n_rows, n_cols, groups, members),
        out_shape=(
            jax.ShapeDtypeStruct((flat, cols), BF16),
            jax.ShapeDtypeStruct((flat, cols), F32),
            jax.ShapeDtypeStruct((LEADS, 2, cols // POOL, channels), F32),
        ),
        in_specs=[hbm] * 11,
        out_specs=(any_space, any_space, vmem),
        scratch_shapes=[
            pltpu.VMEM((4 * channels, both), BF16),
            pltpu.VMEM((3, 3, both), F32),
            pltpu.VMEM((1, 4 * channels), F32),
            pltpu.VMEM((channels, 3 * channels), BF16),
            pltpu.VMEM((1, channels), F32),
            pltpu.VMEM((channels, channels), BF16),
            pltpu.VMEM((32, POOL * cols), BF16),
            pltpu.VMEM((LEADS, flat, cols), BF16),
            pltpu.VMEM((flat, cols), BF16),
            pltpu.VMEM((flat, cols), F32),
            pltpu.VMEM((flat, cols), F32),
            pltpu.VMEM((row_count + 4, both, cols), F32),
            pltpu.VMEM((row_count + 2, both, cols), F32),
            pltpu.VMEM((9, both, cols), F32),
            pltpu.VMEM((9, 2 * both, 2 * cols), BF16),
            pltpu.VMEM((8, 2 * both, 2 * cols), BF16),
            pltpu.VMEM((4 * channels, 2 * both), BF16),
            pltpu.VMEM((both, POOL * cols), BF16),
            pltpu.VMEM((2, 5 * channels, cols), BF16),
            pltpu.VMEM((2, 5 * channels, cols), BF16),
            pltpu.VMEM((2, channels, cols), F32),
            pltpu.VMEM((2, channels, cols), F32),
            pltpu.VMEM((3, 16, both), BF16),
            pltpu.VMEM((6, 3, 16, both), BF16),
            pltpu.VMEM((both, cols), BF16),
            pltpu.VMEM((32, both), BF16),
            pltpu.VMEM((2, 32, both), BF16),
            pltpu.VMEM((32, both), F32),
            pltpu.VMEM((3, both, both), BF16),
            pltpu.VMEM((both, both), BF16),
            pltpu.VMEM((LEADS, members, 2, both), F32),
            pltpu.VMEM((LEADS, members, 2, both), F32),
            pltpu.VMEM((LEADS, groups // DEEP, DEEP, 2 * members, both), BF16),
            pltpu.VMEM((LEADS, members, 2, both), F32),
            pltpu.VMEM((LEADS, members, 2, both), F32),
            dma((15,)),
            dma((4,)),
            dma((4,)),
            dma((LEADS,)),
            dma((LEADS,)),
            dma((LEADS,)),
            dma((LEADS,)),
            dma((LEADS,)),
            dma((LEADS,)),
            dma((LEADS,)),
            dma((LEADS,)),
        ],
        compiler_params=pltpu.CompilerParams(
            collective_id=0, has_side_effects=True, vmem_limit_bytes=60 * 2**20
        ),
    )(
        frames.reshape(LEADS, flat, cols),
        hidden_state.reshape(flat, cols),
        cell_state.reshape(flat, cols),
        jnp.asarray(spreader(cols), BF16),
        jnp.asarray(picker(cols), BF16),
        jnp.transpose(depth_kernel, (1, 2, 0)),
        point_weight,
        gate_bias[None],
        mixing_weight.T,
        query_gain[None],
        output_weight,
    )
    attended, cell, hidden = finish(attended, cell, hidden)
    attended = jnp.transpose(attended, (0, 3, 1, 2))
    shape = (channels, row_count, cols)
    return (hidden.reshape(shape), cell.reshape(shape), attended)


def solution(mesh):
    in_specs = (
        P(None, None, "rows", "cols"),
        P(None, "rows", "cols"),
        P(None, "rows", "cols"),
        P(),
        P(),
        P(),
        P(),
        P(),
        P(),
    )
    out_specs = (P(None, "rows", "cols"), P(None, "rows", "cols"), P(None, None, "rows", "cols"))
    return jax.shard_map(body, mesh=mesh, in_specs=in_specs, out_specs=out_specs, check_vma=False)
```
